256 devices in a mesh: seq: 16 (over z, x_hi), tp: 16 (over y, x_lo, core).
Axes of the slice: x: 4 (x_hi: 2, x_lo: 2; x = x_hi * 2 + x_lo), y: 4, z: 8, core: 2. Of those that a mesh axis runs over, the one named last changes fastest.
Arguments:
- inputs: bfloat16 [8192, 2048], P('seq', 'tp'), may hold values from -6 to 6
- kernel: bfloat16 [8192, 2048], P('seq', 'tp'), may hold values from -6 to 6
- first_blocks: bfloat16 [8192, 512], P('seq'), may hold values from -0.25 to 0.25
- first_cross: bfloat16 [512, 256], P('seq'), may hold values from -1.5 to 1.5
- second_cross: bfloat16 [512, 256], P('seq'), may hold values from -1.5 to 1.5
- second_blocks: bfloat16 [8192, 512], P('seq'), may hold values from -0.25 to 0.25
- gate_weight: bfloat16 [2048, 8192], P('seq', 'tp'), may hold values from -0.125 to 0.125
- up_weight: bfloat16 [2048, 8192], P('seq', 'tp'), may hold values from -0.125 to 0.125
- down_weight: bfloat16 [8192, 2048], P('tp', 'seq'), may hold values from -0.0625 to 0.0625
- cotangent: bfloat16 [8192, 2048], P('seq', 'tp'), may hold values from -6 to 6
Outputs:
- output: bfloat16 [8192, 2048], P('seq', 'tp')
- grad_inputs: bfloat16 [8192, 2048], P('seq', 'tp')
- grad_kernel: bfloat16 [8192, 2048], P('seq', 'tp')
- grad_gate: bfloat16 [2048, 8192], P('seq', 'tp')
- grad_up: bfloat16 [2048, 8192], P('seq', 'tp')
- grad_down: bfloat16 [8192, 2048], P('tp', 'seq')
The draws below stay inside these ranges and needn't reach their ends.
All inputs are finite; a program needn't handle non-finite values.
Results may differ from the reference program's by a relative error of at most 0.025.
Values may be sent and summed in bfloat16 or wider, within the bound.
A program may use at most 64 MiB of HBM per device.

```python
import math
import jax
import jax.numpy as jnp
from jax import lax

D = 2048
FF = 8192
S_DEV = 512
TOKENS = 8192
BLOCKS = 16
N_SEQ = 16
N_TP = 16


def raised(drawn, key, source, target, parts, factor):
    owner, partner = [(jnp.arange(drawn.shape[position]) // (drawn.shape[position] // parts)).reshape([-1 if axis == position else 1 for axis in range(drawn.ndim)]) for position in (source, target)]
    chosen = jax.random.permutation(key, parts)[partner]
    strong = (owner == chosen) | (owner == (partner + parts // 2) % parts)
    return jnp.where(strong, factor * drawn, drawn)


def steps_of(stream_key, extent, pieces, smallest, largest):
    def one(dim, blocks):
        steps = jax.random.uniform(jax.random.fold_in(jax.random.fold_in(stream_key, 6), dim), (blocks,), jnp.float32, smallest / len(pieces), largest / len(pieces))
        return jnp.repeat(jnp.exp(steps), extent[dim] // blocks).reshape((-1,) + (1,) * (len(extent) - dim - 1))

    gain = one(*pieces[0])
    for cut in pieces[1:]:
        gain = gain * one(*cut)
    return gain


def bell_draw(own_key, dims, deviation, most, split=(), kind=jnp.bfloat16):
    drawn = jax.random.normal(own_key, dims, jnp.float32) * deviation
    if len(split) > 0:
        drawn = steps_of(own_key, dims, split, -0.22, 0.18) * drawn
    return jnp.clip(drawn, min=-most, max=most).astype(kind)


def heavy_noise(stream_key, extent, deviation, most, split, heavy, kind=jnp.bfloat16):
    array = deviation * jax.random.normal(stream_key, extent, jnp.float32)
    if split:
        array = array * steps_of(stream_key, extent, split, -0.22, 0.18)
    return jnp.clip(raised(array, jax.random.fold_in(stream_key, 3), *heavy), -most, most).astype(kind)


def setup_inputs(seed: int = 0) -> dict:
    arg_keys = jax.random.split(jax.random.key(seed), 11)
    inputs = bell_draw(arg_keys[0], (TOKENS, D), 1.0, 6.0, ((0, 16), (1, 16)))
    kernel = bell_draw(arg_keys[1], (TOKENS, D), 1.0, 6.0, ((0, 16), (1, 16)))
    first_blocks = bell_draw(arg_keys[2], (TOKENS, S_DEV), S_DEV ** -0.5, 0.25, ((0, 16),))
    first_cross = bell_draw(arg_keys[3], (S_DEV, BLOCKS * BLOCKS), N_SEQ ** -0.5, 1.5, ((0, 16),))
    second_cross = bell_draw(arg_keys[4], (S_DEV, BLOCKS * BLOCKS), N_SEQ ** -0.5, 1.5, ((0, 16),))
    second_blocks = bell_draw(arg_keys[5], (TOKENS, S_DEV), S_DEV ** -0.5, 0.25, ((0, 16),))
    gate_weight = bell_draw(arg_keys[6], (D, FF), D ** -0.5, 0.125, ((0, 16), (1, 16)))
    up_weight = bell_draw(arg_keys[7], (D, FF), D ** -0.5, 0.125, ((0, 16), (1, 16)))
    down_weight = bell_draw(arg_keys[8], (FF, D), FF ** -0.5, 0.0625, ((0, 16), (1, 16)))
    cotangent = heavy_noise(arg_keys[9], (TOKENS, D), 1.0, 6.0, ((0, 16), (1, 16)), (0, 1, 16, 2.0))
    return dict(inputs=inputs, kernel=kernel, first_blocks=first_blocks, first_cross=first_cross, second_cross=second_cross, second_blocks=second_blocks, gate_weight=gate_weight, up_weight=up_weight, down_weight=down_weight, cotangent=cotangent)


def rounded(value):
    return lax.optimization_barrier(value.astype(jnp.bfloat16)).astype(jnp.float32)

def reference(inputs, kernel, first_blocks, first_cross, second_cross, second_blocks, gate_weight, up_weight, down_weight, cotangent):
    groups = N_SEQ
    source = inputs.astype(jnp.float32).reshape(groups, S_DEV, D)
    left_one = first_blocks.astype(jnp.float32).reshape(groups, S_DEV, S_DEV)
    left_two = second_blocks.astype(jnp.float32).reshape(groups, S_DEV, S_DEV)
    cross_one = first_cross.astype(jnp.float32).reshape(S_DEV, groups, groups)
    cross_two = second_cross.astype(jnp.float32).reshape(S_DEV, groups, groups)
    spectral = kernel.astype(jnp.float32).reshape(groups, S_DEV, D)
    inner_mix = jnp.einsum('pts,psc->ptc', left_one, source).astype(jnp.bfloat16)
    crossed = jnp.einsum('tqp,ptc->qtc', cross_one, inner_mix.astype(jnp.float32)).astype(jnp.bfloat16)
    scaled = (spectral * crossed.astype(jnp.float32)).astype(jnp.bfloat16)
    mixed_out = jnp.einsum('tuq,qtc->utc', cross_two, scaled.astype(jnp.float32)).astype(jnp.bfloat16)
    branch = jnp.einsum('ust,utc->usc', left_two, mixed_out.astype(jnp.float32))
    hidden_in = (source + branch).astype(jnp.bfloat16).reshape(TOKENS, D)
    gate_proj = jnp.dot(hidden_in, gate_weight, preferred_element_type=jnp.float32)
    up_proj = jnp.dot(hidden_in, up_weight, preferred_element_type=jnp.float32)
    sig_gate = jax.nn.sigmoid(gate_proj)
    hidden = (gate_proj * sig_gate * up_proj).astype(jnp.bfloat16)
    block_width = FF // N_TP

    def down_part(running, block_index):
        cols = lax.dynamic_slice_in_dim(hidden, block_index * block_width, block_width, 1)
        weights = lax.dynamic_slice_in_dim(down_weight, block_index * block_width, block_width, 0)
        return (running + rounded(jnp.dot(cols, weights, preferred_element_type=jnp.float32)), None)
    down_sum, _ = lax.scan(down_part, jnp.zeros((TOKENS, D), jnp.float32), jnp.arange(N_TP, dtype=jnp.int32))
    output = (hidden_in.astype(jnp.float32) + down_sum).astype(jnp.bfloat16)
    back_hidden = jnp.dot(cotangent, down_weight.T, preferred_element_type=jnp.float32)
    back_gate = (back_hidden * up_proj * sig_gate * (1.0 + gate_proj * (1.0 - sig_gate))).astype(jnp.bfloat16)
    back_up = (back_hidden * gate_proj * sig_gate).astype(jnp.bfloat16)

    def back_part(running, block_index):
        start = block_index * block_width
        gate_cols = lax.dynamic_slice_in_dim(back_gate, start, block_width, 1)
        up_cols = lax.dynamic_slice_in_dim(back_up, start, block_width, 1)
        gate_rows = lax.dynamic_slice_in_dim(gate_weight, start, block_width, 1)
        up_rows = lax.dynamic_slice_in_dim(up_weight, start, block_width, 1)
        partial_value = jnp.dot(gate_cols, gate_rows.T, preferred_element_type=jnp.float32)
        partial_value = partial_value + jnp.dot(up_cols, up_rows.T, preferred_element_type=jnp.float32)
        return (running + rounded(partial_value), None)
    back_sum, _ = lax.scan(back_part, jnp.zeros((TOKENS, D), jnp.float32), jnp.arange(N_TP, dtype=jnp.int32))
    back_total = cotangent.astype(jnp.float32) + back_sum
    grad_scale = 1.0 / math.sqrt(TOKENS)

    def token_part(carry, block_index):
        start = block_index * S_DEV
        feat_rows = lax.dynamic_slice_in_dim(hidden_in, start, S_DEV, 0)
        hid_rows = lax.dynamic_slice_in_dim(hidden, start, S_DEV, 0)
        gate_rows = lax.dynamic_slice_in_dim(back_gate, start, S_DEV, 0)
        up_rows = lax.dynamic_slice_in_dim(back_up, start, S_DEV, 0)
        cot_rows = lax.dynamic_slice_in_dim(cotangent, start, S_DEV, 0)
        part_gate = rounded(jnp.dot(feat_rows.T, gate_rows, preferred_element_type=jnp.float32) * grad_scale)
        part_up = rounded(jnp.dot(feat_rows.T, up_rows, preferred_element_type=jnp.float32) * grad_scale)
        part_down = rounded(jnp.dot(hid_rows.T, cot_rows, preferred_element_type=jnp.float32) * grad_scale)
        return ((carry[0] + part_gate, carry[1] + part_up, carry[2] + part_down), None)
    start_sums = (jnp.zeros((D, FF), jnp.float32), jnp.zeros((D, FF), jnp.float32), jnp.zeros((FF, D), jnp.float32))
    sums, _ = lax.scan(token_part, start_sums, jnp.arange(groups, dtype=jnp.int32))
    grad_gate = sums[0].astype(jnp.bfloat16)
    grad_up = sums[1].astype(jnp.bfloat16)
    grad_down = sums[2].astype(jnp.bfloat16)
    total_blocks = back_total.reshape(groups, S_DEV, D)
    back_branch = total_blocks.astype(jnp.bfloat16).astype(jnp.float32)
    back_mixed = jnp.einsum('ust,usc->utc', left_two, back_branch).astype(jnp.bfloat16)
    back_scaled = jnp.einsum('tuq,utc->qtc', cross_two, back_mixed.astype(jnp.float32)).astype(jnp.bfloat16)
    grad_kernel = (back_scaled.astype(jnp.float32) * crossed.astype(jnp.float32)).astype(jnp.bfloat16)
    back_crossed = (back_scaled.astype(jnp.float32) * spectral).astype(jnp.bfloat16)
    back_inner = jnp.einsum('tqp,qtc->ptc', cross_one, back_crossed.astype(jnp.float32)).astype(jnp.bfloat16)
    back_source = jnp.einsum('pts,ptc->psc', left_one, back_inner.astype(jnp.float32))
    grad_inputs = (total_blocks + back_source).astype(jnp.bfloat16).reshape(TOKENS, D)
    return (output, grad_inputs, grad_kernel.reshape(TOKENS, D), grad_gate, grad_up, grad_down)
```

```python
import math

import jax
import jax.numpy as jnp
from jax import lax
from jax.experimental import pallas as pl
from jax.experimental.pallas import tpu as pltpu
from jax.sharding import PartitionSpec as P

MESH = pl.DeviceIdType.MESH
BF = jnp.bfloat16
F32 = jnp.float32
MIB = 1 << 20
N_SEM = 512


def dot(a, b):
    return jnp.dot(a, b, preferred_element_type=F32)


def dot_nt(a, b):
    return lax.dot_general(a, b, (((1,), (1,)), ((), ())), preferred_element_type=F32)


def rem(a, n):
    return lax.rem(a, jnp.int32(n))


def div(a, n):
    return lax.div(a, jnp.int32(n))


def mo(v, n):
    return pl.multiple_of(v, n)


def layer_kernel(
    x, kk, a1, c1, c2, a2, wg, wu, wd, cot,
    out, grad_in, grad_k, o_gate, o_up, o_down,
    wgf, wuf, wdf, feat, cotf,
    m1, m1t, m2, m2t, a1t, a2t,
    inner, spread, kspread, crossed, mixed, mhome, hid_in,
    bh, hidden, bgate, bup, bt, dt,
    gg, gu, gd, coregot, rsum,
    zr, swap_src, swap_got, r1, r2, r3, r4, rhome, total,
    bmix, bspread, gks, binner, ihome, gkhome,
    ssem, rsem,
):
    s = lax.axis_index("seq")
    t = lax.axis_index("tp")
    z, h = div(s, 2), rem(s, 2)
    y, l, c = div(t, 4), rem(div(t, 2), 2), rem(t, 2)
    xx = h * 2 + l
    own_side = c == h

    def seq_dev(j):
        return {"seq": j, "tp": t}

    def z_dev(d):
        return {"seq": rem(z + (8 + d), 8) * 2 + h, "tp": t}

    def plane(yy, xp):
        return {"seq": z * 2 + div(xp, 2), "tp": yy * 4 + rem(xp, 2) * 2 + c}

    core_dev = {"seq": s, "tp": t + 1 - 2 * c}
    swap_dev = {"seq": z * 2 + 1 - h, "tp": t + 1 - 2 * c}

    def nb(axis, d):
        if axis == "y":
            return plane(rem(y + (4 + d), 4), xx)
        return plane(y, rem(xx + (4 + d), 4))

    count = [0]
    sends = []

    def remote(src, dst, dev):
        i = count[0]
        count[0] += 1
        return pltpu.make_async_remote_copy(
            src, dst, ssem.at[i], rsem.at[i], device_id=dev, device_id_type=MESH
        )

    def send(src, dst, dev):
        copy = remote(src, dst, dev)
        copy.start()
        sends.append(copy.wait_send)
        return copy

    def exchange_order(i):
        k = div(i + 1, 2)
        return 8 + k * (2 * rem(i + 1, 2) - 1)

    def exchange(src, dst):
        base = count[0]
        count[0] += 15

        def copy(i):
            j = rem(s + exchange_order(i), 16)
            return pltpu.make_async_remote_copy(
                src.at[pl.ds(mo(j * 32, 32), 32)],
                dst.at[pl.ds(mo(s * 32, 32), 32)],
                ssem.at[base + i], rsem.at[base + i],
                device_id=seq_dev(j), device_id_type=MESH,
            )

        def over(act):
            def step(i, carry):
                act(copy(i))
                return carry
            lax.fori_loop(0, 15, step, 0)

        over(lambda p: p.start())
        mine = pl.ds(mo(s * 32, 32), 32)
        dst[mine, :] = src[mine, :]
        sends.append(lambda: over(lambda p: p.wait_send()))
        return lambda: over(lambda p: p.wait_recv())

    def slot(ref, a, first, f, g, r0, nr):
        yy, xp = (f, g) if first == "y" else (g, f)
        rows = div(xp, 2) * 256 + (a * 128 + r0)
        cols = (yy * 2 + rem(xp, 2)) * 256
        return ref.at[pl.ds(mo(rows, 64), nr), pl.ds(mo(cols, 256), 256)]

    def axes_of(first):
        return (y, xx, "x") if first == "y" else (xx, y, "y")

    def gather_plane(buf):
        halves = ((0, "y"), (1, "x"))
        st1, st2 = {}, {}

        def second(a, first, di):
            p1, p2, other = axes_of(first)
            f = rem(p1 + (4 + di), 4)
            piece = slot(buf, a, first, f, p2, 0, 128)
            st2[a, di] = [send(piece, piece, nb(other, d)) for d in (1, -1)]

        def second_forward(a, first, di):
            p1, p2, other = axes_of(first)
            f = rem(p1 + (4 + di), 4)
            got = []
            for k, d in ((0, 1), (1, -1)):
                st2[a, di][k].wait_recv()
                piece = slot(buf, a, first, f, rem(p2 + (4 - d), 4), k * 64, 64)
                got.append(send(piece, piece, nb(other, d)))
            st2[a, di] = got

        for a, first in halves:
            p1, p2, _ = axes_of(first)
            piece = slot(buf, a, first, p1, p2, 0, 128)
            st1[a] = [send(piece, piece, nb(first, d)) for d in (1, -1)]
        for a, first in halves:
            second(a, first, 0)
        yield
        fwd = {}
        for a, first in halves:
            p1, p2, _ = axes_of(first)
            fwd[a] = []
            for k, d in ((0, 1), (1, -1)):
                st1[a][k].wait_recv()
                piece = slot(buf, a, first, rem(p1 + (4 - d), 4), p2, k * 64, 64)
                fwd[a].append(send(piece, piece, nb(first, d)))
        for a, first in halves:
            second(a, first, -1)
            second(a, first, 1)
        yield
        for a, first in halves:
            second_forward(a, first, 0)
        yield
        for a, first in halves:
            for copy in fwd[a]:
                copy.wait_recv()
            second(a, first, 2)
        yield
        for di in (-1, 1):
            for a, first in halves:
                second_forward(a, first, di)
        yield
        for a, first in halves:
            second_forward(a, first, 2)
        yield
        for di in (0, -1, 1, 2):
            for a, first in halves:
                for copy in st2[a, di]:
                    copy.wait_recv()

    def add_into(ref, *others):
        value = ref[...].astype(F32)
        for other in others:
            value = value + other[...].astype(F32)
        ref[...] = value.astype(BF)

    def scatter_plane(buf, w):
        halves = ((0, "x"), (1, "y"))
        order = (2, 1, -1, 0)
        st1, st2, st3, st4 = {}, {}, {}, {}
        for gi, dg in enumerate(order):
            for a, first in halves:
                p1, p2, _ = axes_of(first)
                f, g = rem(p1 + 2, 4), rem(p2 + (4 + dg), 4)
                st1[a, gi] = [
                    send(
                        slot(buf, a, first, f, g, k * 64, 64), r1.at[w, a, gi, k], nb(first, d)
                    )
                    for k, d in ((0, 1), (1, -1))
                ]
        yield
        for gi, dg in enumerate(order):
            for a, first in halves:
                p1, p2, _ = axes_of(first)
                g = rem(p2 + (4 + dg), 4)
                st2[a, gi] = []
                for k, d in ((0, 1), (1, -1)):
                    st1[a, gi][k].wait_recv()
                    f = rem(p1 + (4 + d), 4)
                    add_into(slot(buf, a, first, f, g, k * 64, 64), r1.at[w, a, gi, k])
                    st2[a, gi].append(
                        send(
                            slot(buf, a, first, f, g, 0, 128), r2.at[w, a, gi, k], nb(first, d)
                        )
                    )
            yield
        for gi, dg in enumerate(order):
            for a, first in halves:
                p1, p2, other = axes_of(first)
                g = rem(p2 + (4 + dg), 4)
                for copy in st2[a, gi]:
                    copy.wait_recv()
                add_into(
                    slot(buf, a, first, p1, g, 0, 128), r2.at[w, a, gi, 0], r2.at[w, a, gi, 1]
                )
                if dg == 2:
                    st3[a] = [
                        send(
                            slot(buf, a, first, p1, g, k * 64, 64), r3.at[w, a, k], nb(other, d)
                        )
                        for k, d in ((0, 1), (1, -1))
                    ]
            yield
        for a, first in halves:
            p1, p2, other = axes_of(first)
            st4[a] = []
            for k, d in ((0, 1), (1, -1)):
                g = rem(p2 + (4 + d), 4)
                st3[a][k].wait_recv()
                add_into(slot(buf, a, first, p1, g, k * 64, 64), r3.at[w, a, k])
                st4[a].append(
                    send(slot(buf, a, first, p1, g, 0, 128), r4.at[w, a, k], nb(other, d))
                )
        yield
        for a, first in halves:
            p1, p2, other = axes_of(first)
            for copy in st4[a]:
                copy.wait_recv()
            add_into(slot(buf, a, first, p1, p2, 0, 128), r4.at[w, a, 0], r4.at[w, a, 1])
        rows = pl.ds(mo(h * 256, 256), 256)
        cols = pl.ds(mo((y * 2 + l) * 256 + (1 - c) * 128, 128), 128)
        back = send(buf.at[rows, cols], rhome.at[w], core_dev)
        yield
        back.wait_recv()

    half_rows = pl.ds(mo(c * 256, 256), 256)
    other_rows = pl.ds(mo((1 - c) * 256, 256), 256)
    my_rows = pl.ds(mo(h * 256, 256), 256)
    my_cols = pl.ds(mo((y * 2 + l) * 256 + c * 128, 128), 128)

    def share_core(src, buf):
        copy = send(src.at[other_rows], buf.at[my_rows, my_cols], core_dev)
        buf[my_rows, my_cols] = src[half_rows, :]
        return copy

    def wslice(w, j, part=None):
        ref = (wdf, wgf, wuf)[w]
        if w == 0:
            rows = pl.ds(0, 512) if part is None else pl.ds(part * 256, 256)
            return ref.at[rows, pl.ds(mo(j * 128, 128), 128)]
        if part is None:
            return ref.at[pl.ds(mo(j * 128, 128), 128), :]
        return ref.at[pl.ds(mo(j * 128 + part * 64, 64), 64), :]

    wsrc = (wd, wg, wu)
    core_waits = []

    def ring_weights():
        swaps = [remote(wsrc[w], wslice(w, s), swap_dev) for w in range(3)]

        @pl.when(jnp.logical_not(own_side))
        def _():
            for copy in swaps:
                copy.start()

        @pl.when(own_side)
        def _():
            for w in range(3):
                wslice(w, s)[...] = wsrc[w][...]

        def wait_swaps():
            @pl.when(jnp.logical_not(own_side))
            def _():
                for copy in swaps:
                    copy.wait_send()

        sends.append(wait_swaps)
        yield
        pend = {}

        def pass_on(w, dz, d, part=None):
            piece = wslice(w, rem(z + (8 + dz), 8) * 2 + c, part)
            pend[w, d] = send(piece, piece, z_dev(d))

        def to_core(w, dz):
            piece = wslice(w, rem(z + (8 + dz), 8) * 2 + c)
            core_waits.append(send(piece, piece, core_dev))

        for w in range(3):
            @pl.when(jnp.logical_not(own_side))
            def _():
                swaps[w].wait_recv()
            pass_on(w, 0, 1)
            pass_on(w, 0, -1)
        for w in range(3):
            to_core(w, 0)
        yield
        for k in (1, 2, 3):
            for w in range(3):
                for d in (1, -1):
                    pend[w, d].wait_recv()
                    part = None if k < 3 else (0 if d == 1 else 1)
                    pass_on(w, -d * k, d, part)
                for d in (1, -1):
                    to_core(w, -d * k)
                yield
        for w in range(3):
            for d in (1, -1):
                pend[w, d].wait_recv()
            to_core(w, 4)
        yield
        for copy in core_waits:
            copy.wait_recv()

    def core_blocks(w, buf):
        return [buf, w]

    gbufs = (gg, gu, gd)
    got_core = {}
    zorder = (4, 3, -3, 2, -2, 1, -1, 0)

    def grad_tiles(w, lhs, rhs, scale):
        lhs_t = lhs[...].T
        for i, dz in enumerate(zorder):
            zz = rem(z + (8 + dz), 8)
            cols = pl.ds(mo(zz * 256, 256), 256)
            gbufs[w][:, cols] = (dot(lhs_t, rhs[:, cols]) * scale).astype(BF)
            there = pl.ds(mo(zz * 256 + (1 - c) * 128, 128), 128)
            got_core[w, i] = send(gbufs[w].at[:, there], coregot.at[w, i], core_dev)

    def mine_block(w, dz, part=None):
        zz = rem(z + (8 + dz), 8)
        cols = pl.ds(mo(zz * 256 + c * 128, 128), 128)
        rows = pl.ds(0, 512) if part is None else pl.ds(part * 256, 256)
        return gbufs[w].at[rows, cols]

    def ring_grads(w):
        for i in (0,):
            got_core[w, i].wait_recv()
            add_into(mine_block(w, 4), coregot.at[w, i])
        pend = [
            send(mine_block(w, 4, k), zr.at[w, 0, k, pl.ds(0, 256)], z_dev(d))
            for k, d in ((0, 1), (1, -1))
        ]
        for i in range(1, 8):
            got_core[w, i].wait_recv()
            add_into(mine_block(w, zorder[i]), coregot.at[w, i])
        yield
        for n in (3, 2, 1):
            new = []
            for k, d in ((0, 1), (1, -1)):
                pend[k].wait_recv()
                if n == 3:
                    add_into(mine_block(w, d * n, k), zr.at[w, 0, k, pl.ds(0, 256)])
                else:
                    add_into(mine_block(w, d * n), zr.at[w, 3 - n, k])
                new.append(send(mine_block(w, d * n), zr.at[w, 4 - n, k], z_dev(d)))
            pend = new
            yield
        for copy in pend:
            copy.wait_recv()
        add_into(mine_block(w, 0), zr.at[w, 3, 0], zr.at[w, 3, 1])
        swap = remote(mine_block(w, 0), swap_got.at[w], swap_dev)

        @pl.when(jnp.logical_not(own_side))
        def _():
            swap.start()

        yield

        @pl.when(jnp.logical_not(own_side))
        def _():
            swap.wait()

        @pl.when(own_side)
        def _():
            swap_got[w] = mine_block(w, 0)[...]

        if w == 0:
            o_gate[...] = swap_got[w].T
        elif w == 1:
            o_up[...] = swap_got[w].T
        else:
            o_down[...] = swap_got[w]

    def run(flow, n=1):
        for _ in range(n):
            next(flow, None)

    def drain(flow):
        for _ in flow:
            pass

    barrier = pltpu.get_barrier_semaphore()
    partners = [seq_dev(rem(s + d, 16)) for d in range(1, 16)]
    partners += [nb("y", 1), nb("y", -1), nb("x", 1), nb("x", -1), core_dev, swap_dev]
    for dev in partners:
        pl.semaphore_signal(barrier, inc=1, device_id=dev, device_id_type=MESH)
    inner[...] = dot(a1[...], x[...]).astype(BF)
    pl.semaphore_wait(barrier, len(partners))

    got_inner = exchange(inner, spread)
    got_k = exchange(kk, kspread)
    weights = ring_weights()
    run(weights)
    got_cot = share_core(cot, cotf)

    row = lax.broadcasted_iota(jnp.int32, (256, 512), 0)
    col = lax.broadcasted_iota(jnp.int32, (256, 512), 1)
    pick = (row == div(col, 32)).astype(F32).astype(BF)
    pick_t = (row == div(col, 32) * 16).astype(F32).astype(BF)
    diag = (
        lax.broadcasted_iota(jnp.int32, (32, 512), 0)
        == rem(lax.broadcasted_iota(jnp.int32, (32, 512), 1), 32)
    ).astype(F32)

    def widen(cross, m, mt):
        values = cross[...].astype(F32)

        def step(i, carry):
            rows = pl.ds(mo(i * 32, 32), 32)
            turned = pltpu.roll(values, 256 - i * 16, 1).astype(BF)
            m[rows, :] = (dot(turned, pick) * diag).astype(BF)
            turned = pltpu.roll(values, 256 - i, 1).astype(BF)
            mt[rows, :] = (dot(turned, pick_t) * diag).astype(BF)
            return carry

        lax.fori_loop(0, 16, step, 0)

    widen(c1, m1, m1t)
    widen(c2, m2, m2t)

    got_cot.wait_recv()
    cot_flow = gather_plane(cotf)
    run(cot_flow)

    got_inner()
    crossed[...] = dot(m1[...], spread[...]).astype(BF)
    got_k()
    scaled = (kspread[...].astype(F32) * crossed[...].astype(F32)).astype(BF)
    mixed[...] = dot(m2[...], scaled).astype(BF)
    got_mixed = exchange(mixed, mhome)
    a1t[...] = a1[...].T
    a2t[...] = a2[...].T
    run(weights)
    run(cot_flow, 2)
    got_mixed()
    hid_in[...] = (x[...].astype(F32) + dot(a2[...], mhome[...])).astype(BF)
    got_feat = share_core(hid_in, feat)
    run(cot_flow)
    got_feat.wait_recv()
    feat_flow = gather_plane(feat)
    run(feat_flow)
    run(weights, 3)
    run(cot_flow)
    run(feat_flow)
    run(cot_flow)
    run(feat_flow)
    drain(cot_flow)
    run(weights, 3)
    run(feat_flow)
    run(weights, 3)
    run(feat_flow)
    run(weights)
    drain(weights)
    for j in range(2):
        cols = pl.ds(j * 256, 256)
        bh[:, cols] = dot_nt(cotf[...], wdf[cols, :])
    drain(feat_flow)

    for j in range(2):
        cols = pl.ds(j * 256, 256)
        gate = dot(feat[...], wgf[:, cols])
        up = dot(feat[...], wuf[:, cols])
        sig = 1.0 / (1.0 + jnp.exp(-gate))
        back = bh[:, cols]
        hidden[:, cols] = (gate * sig * up).astype(BF)
        bgate[:, cols] = (back * up * sig * (1.0 + gate * (1.0 - sig))).astype(BF)
        bup[:, cols] = (back * gate * sig).astype(BF)
    for j in range(8):
        rows = pl.ds(j * 256, 256)
        bt[:, rows] = (dot_nt(bgate[...], wgf[rows, :]) + dot_nt(bup[...], wuf[rows, :])).astype(BF)
    back_flow = scatter_plane(bt, 0)
    run(back_flow)
    scale = 1.0 / math.sqrt(8192.0)
    grad_tiles(0, bgate, feat, scale)
    run(back_flow, 4)
    grads = [ring_grads(w) for w in range(3)]
    run(grads[0])
    grad_tiles(1, bup, feat, scale)
    run(back_flow, 4)
    run(grads[1])
    grad_tiles(2, hidden, cotf, scale)
    run(back_flow)
    run(grads[0])
    run(grads[2])
    run(back_flow)
    for j in range(8):
        cols = pl.ds(j * 256, 256)
        dt[:, cols] = dot(hidden[...], wdf[:, cols]).astype(BF)
    drain(back_flow)
    down_flow = scatter_plane(dt, 1)
    run(down_flow)

    total[half_rows, :] = cot[half_rows, :].astype(F32) + bt[my_rows, my_cols].astype(F32)
    total[other_rows, :] = cot[other_rows, :].astype(F32) + rhome[0].astype(F32)
    bmix[...] = dot(a2t[...], total[...].astype(BF)).astype(BF)
    got_back = exchange(bmix, bspread)
    for w in (1, 0, 2, 1):
        run(grads[w])
    run(down_flow, 4)
    got_back()
    bscaled = dot(m2t[...], bspread[...]).astype(BF).astype(F32)
    bcrossed = (bscaled * kspread[...].astype(F32)).astype(BF)
    gks[...] = (bscaled * crossed[...].astype(F32)).astype(BF)
    binner[...] = dot(m1t[...], bcrossed).astype(BF)
    got_binner = exchange(binner, ihome)
    got_gk = exchange(gks, gkhome)
    for w in (0, 2, 1):
        run(grads[w])
    run(down_flow, 4)
    for w in (0, 2):
        run(grads[w])
    got_binner()
    grad_in[...] = (total[...] + dot(a1t[...], ihome[...])).astype(BF)
    run(down_flow)
    got_gk()
    grad_k[...] = gkhome[...]
    run(down_flow)
    for w in (0, 1, 2):
        run(grads[w])
    drain(down_flow)
    out[half_rows, :] = (
        hid_in[half_rows, :].astype(F32) + dt[my_rows, my_cols].astype(F32)
    ).astype(BF)
    out[other_rows, :] = (hid_in[other_rows, :].astype(F32) + rhome[1].astype(F32)).astype(BF)
    for w in (0, 1, 2):
        drain(grads[w])
    for wait in sends:
        wait()
    assert count[0] <= N_SEM, count[0]


def per_device(*args):
    vm = pltpu.VMEM
    scratch = [
        vm((2048, 512), BF), vm((2048, 512), BF), vm((512, 2048), BF),
        vm((512, 2048), BF), vm((512, 2048), BF),
    ]
    scratch += [vm((512, 512), BF)] * 6
    scratch += [vm((512, 128), BF)] * 7
    scratch += [vm((512, 512), F32)] + [vm((512, 512), BF)] * 3
    scratch += [vm((512, 2048), BF)] * 2
    scratch += [vm((512, 2048), BF)] * 3
    scratch += [vm((3, 8, 512, 128), BF), vm((16, 128), BF)]
    scratch += [
        vm((3, 4, 2, 512, 128), BF), vm((16, 128), BF), vm((3, 512, 128), BF),
        vm((2, 2, 4, 2, 64, 256), BF), vm((2, 2, 4, 2, 128, 256), BF),
        vm((2, 2, 2, 64, 256), BF), vm((2, 2, 2, 128, 256), BF),
        vm((2, 256, 128), BF), vm((512, 128), F32),
    ]
    scratch += [vm((512, 128), BF)] * 6
    scratch += [pltpu.SemaphoreType.DMA((N_SEM,)), pltpu.SemaphoreType.DMA((N_SEM,))]
    wide = jax.ShapeDtypeStruct((512, 128), BF)
    tall = jax.ShapeDtypeStruct((128, 512), BF)
    return pl.pallas_call(
        layer_kernel,
        name="mixer_layer",
        out_shape=[wide, wide, wide, tall, tall, wide],
        in_specs=[pl.BlockSpec(memory_space=vm)] * 10,
        out_specs=[pl.BlockSpec(memory_space=vm)] * 6,
        scratch_shapes=scratch,
        compiler_params=pltpu.CompilerParams(
            collective_id=0, has_side_effects=True, vmem_limit_bytes=56 * MIB
        ),
    )(*args)


def solution(mesh):
    return jax.shard_map(
        per_device,
        mesh=mesh,
        in_specs=(
            P("seq", "tp"),
            P("seq", "tp"),
            P("seq", None),
            P("seq", None),
            P("seq", None),
            P("seq", None),
            P("seq", "tp"),
            P("seq", "tp"),
            P("tp", "seq"),
            P("seq", "tp"),
        ),
        out_specs=(
            P("seq", "tp"),
            P("seq", "tp"),
            P("seq", "tp"),
            P("seq", "tp"),
            P("seq", "tp"),
            P("tp", "seq"),
        ),
        check_vma=False,
    )
```

```python
import math

import jax
import jax.numpy as jnp
from jax import lax
from jax.experimental import pallas as pl
from jax.experimental.pallas import tpu as pltpu
from jax.sharding import PartitionSpec as P

MESH = pl.DeviceIdType.MESH
BF = jnp.bfloat16
F32 = jnp.float32
MIB = 1 << 20
N_SEM = 512


def dot(a, b):
    return jnp.dot(a, b, preferred_element_type=F32)


def dot_nt(a, b):
    return lax.dot_general(a, b, (((1,), (1,)), ((), ())), preferred_element_type=F32)


def rem(a, n):
    return lax.rem(a, jnp.int32(n))


def div(a, n):
    return lax.div(a, jnp.int32(n))


def mo(v, n):
    return pl.multiple_of(v, n)


def layer_kernel(
    x, kk, a1, c1, c2, a2, wg, wu, wd, cot,
    out, grad_in, grad_k, o_gate, o_up, o_down,
    wgf, wuf, wdf, feat, cotf,
    m1, m1t, m2, m2t, a1t, a2t,
    inner, spread, kspread, crossed, mixed, mhome, hid_in,
    bh, hidden, bgate, bup, bt, dt,
    gg, gu, gd, coregot, turned, lhs_t,
    zr, swap_got, r1, r2, r3, r4, rhome, total,
    bmix, bspread, gks, binner, ihome, gkhome,
    ssem, rsem,
):
    s = lax.axis_index("seq")
    t = lax.axis_index("tp")
    z, h = div(s, 2), rem(s, 2)
    y, l, c = div(t, 4), rem(div(t, 2), 2), rem(t, 2)
    xx = h * 2 + l
    own_side = c == h

    def seq_dev(j):
        return {"seq": j, "tp": t}

    def z_dev(d):
        return {"seq": rem(z + (8 + d), 8) * 2 + h, "tp": t}

    def plane(yy, xp):
        return {"seq": z * 2 + div(xp, 2), "tp": yy * 4 + rem(xp, 2) * 2 + c}

    core_dev = {"seq": s, "tp": t + 1 - 2 * c}
    swap_dev = {"seq": z * 2 + 1 - h, "tp": t + 1 - 2 * c}

    def nb(axis, d):
        if axis == "y":
            return plane(rem(y + (4 + d), 4), xx)
        return plane(y, rem(xx + (4 + d), 4))

    count = [0]
    sends = []

    def remote(src, dst, dev):
        i = count[0]
        count[0] += 1
        return pltpu.make_async_remote_copy(
            src, dst, ssem.at[i], rsem.at[i], device_id=dev, device_id_type=MESH
        )

    def send(src, dst, dev):
        copy = remote(src, dst, dev)
        copy.start()
        sends.append(copy.wait_send)
        return copy

    def exchange_order(i):
        k = div(i + 1, 2)
        return 8 + k * (2 * rem(i + 1, 2) - 1)

    def exchange(src, dst):
        base = count[0]
        count[0] += 15

        def copy(i):
            j = rem(s + exchange_order(i), 16)
            return pltpu.make_async_remote_copy(
                src.at[pl.ds(mo(j * 32, 32), 32)],
                dst.at[pl.ds(mo(s * 32, 32), 32)],
                ssem.at[base + i], rsem.at[base + i],
                device_id=seq_dev(j), device_id_type=MESH,
            )

        def over(act):
            def step(i, carry):
                act(copy(i))
                return carry
            lax.fori_loop(0, 15, step, 0)

        over(lambda p: p.start())
        mine = pl.ds(mo(s * 32, 32), 32)
        dst[mine, :] = src[mine, :]
        sends.append(lambda: over(lambda p: p.wait_send()))
        return lambda: over(lambda p: p.wait_recv())

    def slot(ref, a, first, f, g, r0, nr):
        yy, xp = (f, g) if first == "y" else (g, f)
        rows = div(xp, 2) * 256 + (a * 128 + r0)
        cols = (yy * 2 + rem(xp, 2)) * 256
        return ref.at[pl.ds(mo(rows, 64), nr), pl.ds(mo(cols, 256), 256)]

    def axes_of(first):
        return (y, xx, "x") if first == "y" else (xx, y, "y")

    def gather_plane(buf):
        halves = ((0, "y"), (1, "x"))
        st1, st2 = {}, {}

        def second(a, first, di):
            p1, p2, other = axes_of(first)
            f = rem(p1 + (4 + di), 4)
            piece = slot(buf, a, first, f, p2, 0, 128)
            st2[a, di] = [send(piece, piece, nb(other, d)) for d in (1, -1)]

        def second_forward(a, first, di):
            p1, p2, other = axes_of(first)
            f = rem(p1 + (4 + di), 4)
            got = []
            for k, d in ((0, 1), (1, -1)):
                st2[a, di][k].wait_recv()
                piece = slot(buf, a, first, f, rem(p2 + (4 - d), 4), k * 64, 64)
                got.append(send(piece, piece, nb(other, d)))
            st2[a, di] = got

        for a, first in halves:
            p1, p2, _ = axes_of(first)
            piece = slot(buf, a, first, p1, p2, 0, 128)
            st1[a] = [send(piece, piece, nb(first, d)) for d in (1, -1)]
        for a, first in halves:
            second(a, first, 0)
        yield
        fwd = {}
        for a, first in halves:
            p1, p2, _ = axes_of(first)
            fwd[a] = []
            for k, d in ((0, 1), (1, -1)):
                st1[a][k].wait_recv()
                piece = slot(buf, a, first, rem(p1 + (4 - d), 4), p2, k * 64, 64)
                fwd[a].append(send(piece, piece, nb(first, d)))
        for a, first in halves:
            second(a, first, -1)
            second(a, first, 1)
        yield
        for a, first in halves:
            second_forward(a, first, 0)
        yield
        for a, first in halves:
            for copy in fwd[a]:
                copy.wait_recv()
            second(a, first, 2)
        yield
        for di in (-1, 1):
            for a, first in halves:
                second_forward(a, first, di)
        yield
        for a, first in halves:
            second_forward(a, first, 2)
        yield
        for di in (0, -1, 1, 2):
            for a, first in halves:
                for copy in st2[a, di]:
                    copy.wait_recv()

    def add_into(ref, *others):
        value = ref[...].astype(F32)
        for other in others:
            value = value + other[...].astype(F32)
        ref[...] = value.astype(BF)

    def scatter_plane(buf, w):
        halves = ((0, "x"), (1, "y"))
        order = (2, 1, -1, 0)
        st1, st2, st3, st4 = {}, {}, {}, {}
        for gi, dg in enumerate(order):
            for a, first in halves:
                p1, p2, _ = axes_of(first)
                f, g = rem(p1 + 2, 4), rem(p2 + (4 + dg), 4)
                st1[a, gi] = [
                    send(
                        slot(buf, a, first, f, g, k * 64, 64), r1.at[w, a, gi, k], nb(first, d)
                    )
                    for k, d in ((0, 1), (1, -1))
                ]
        yield
        for gi, dg in enumerate(order):
            for a, first in halves:
                p1, p2, _ = axes_of(first)
                g = rem(p2 + (4 + dg), 4)
                st2[a, gi] = []
                for k, d in ((0, 1), (1, -1)):
                    st1[a, gi][k].wait_recv()
                    f = rem(p1 + (4 + d), 4)
                    add_into(slot(buf, a, first, f, g, k * 64, 64), r1.at[w, a, gi, k])
                    st2[a, gi].append(
                        send(
                            slot(buf, a, first, f, g, 0, 128), r2.at[w, a, gi, k], nb(first, d)
                        )
                    )
            yield
        for gi, dg in enumerate(order):
            for a, first in halves:
                p1, p2, other = axes_of(first)
                g = rem(p2 + (4 + dg), 4)
                for copy in st2[a, gi]:
                    copy.wait_recv()
                add_into(
                    slot(buf, a, first, p1, g, 0, 128), r2.at[w, a, gi, 0], r2.at[w, a, gi, 1]
                )
                if dg == 2:
                    st3[a] = [
                        send(
                            slot(buf, a, first, p1, g, k * 64, 64), r3.at[w, a, k], nb(other, d)
                        )
                        for k, d in ((0, 1), (1, -1))
                    ]
            yield
        for a, first in halves:
            p1, p2, other = axes_of(first)
            st4[a] = []
            for k, d in ((0, 1), (1, -1)):
                g = rem(p2 + (4 + d), 4)
                st3[a][k].wait_recv()
                add_into(slot(buf, a, first, p1, g, k * 64, 64), r3.at[w, a, k])
                st4[a].append(
                    send(slot(buf, a, first, p1, g, 0, 128), r4.at[w, a, k], nb(other, d))
                )
        yield
        for a, first in halves:
            p1, p2, other = axes_of(first)
            for copy in st4[a]:
                copy.wait_recv()
            add_into(slot(buf, a, first, p1, p2, 0, 128), r4.at[w, a, 0], r4.at[w, a, 1])
        rows = pl.ds(mo(h * 256, 256), 256)
        cols = pl.ds(mo((y * 2 + l) * 256 + (1 - c) * 128, 128), 128)
        back = send(buf.at[rows, cols], rhome.at[w], core_dev)
        yield
        back.wait_recv()

    half_rows = pl.ds(mo(c * 256, 256), 256)
    other_rows = pl.ds(mo((1 - c) * 256, 256), 256)
    my_rows = pl.ds(mo(h * 256, 256), 256)
    my_cols = pl.ds(mo((y * 2 + l) * 256 + c * 128, 128), 128)

    def share_core(src, buf):
        copy = send(src.at[other_rows], buf.at[my_rows, my_cols], core_dev)
        buf[my_rows, my_cols] = src[half_rows, :]
        return copy

    def wslice(w, j, part=None):
        ref = (wdf, wgf, wuf)[w]
        if w == 0:
            rows = pl.ds(0, 512) if part is None else pl.ds(part * 256, 256)
            return ref.at[rows, pl.ds(mo(j * 128, 128), 128)]
        if part is None:
            return ref.at[pl.ds(mo(j * 128, 128), 128), :]
        return ref.at[pl.ds(mo(j * 128 + part * 64, 64), 64), :]

    wsrc = (wd, wg, wu)
    core_waits = []

    def ring_weights():
        swaps = [remote(wsrc[w], wslice(w, s), swap_dev) for w in range(3)]
        pend = {}
        first = {}
        for w in range(3):
            piece = wslice(w, z * 2 + c)
            pend[w, 1] = remote(piece, piece, z_dev(1))
            pend[w, -1] = remote(piece, piece, z_dev(-1))
            first[w] = [pend[w, 1], pend[w, -1], remote(piece, piece, core_dev)]
            for copy in first[w]:
                sends.append(copy.wait_send)
            core_waits.append(first[w][2])

        @pl.when(jnp.logical_not(own_side))
        def _():
            for copy in swaps:
                copy.start()

        @pl.when(own_side)
        def _():
            for w in range(3):
                wslice(w, s)[...] = wsrc[w][...]
                for copy in first[w]:
                    copy.start()

        def wait_swaps():
            @pl.when(jnp.logical_not(own_side))
            def _():
                for copy in swaps:
                    copy.wait_send()

        sends.append(wait_swaps)
        yield

        def pass_on(w, dz, d, part=None):
            piece = wslice(w, rem(z + (8 + dz), 8) * 2 + c, part)
            pend[w, d] = send(piece, piece, z_dev(d))

        def to_core(w, dz):
            piece = wslice(w, rem(z + (8 + dz), 8) * 2 + c)
            core_waits.append(send(piece, piece, core_dev))

        @pl.when(jnp.logical_not(own_side))
        def _():
            for w in range(3):
                swaps[w].wait_recv()
                for copy in first[w]:
                    copy.start()

        yield
        for k in (1, 2, 3):
            for w in range(3):
                for d in (1, -1):
                    pend[w, d].wait_recv()
                    part = None if k < 3 else (0 if d == 1 else 1)
                    pass_on(w, -d * k, d, part)
                for d in (1, -1):
                    to_core(w, -d * k)
                yield
        for w in range(3):
            for d in (1, -1):
                pend[w, d].wait_recv()
            to_core(w, 4)
        yield
        for copy in core_waits:
            copy.wait_recv()

    gbufs = (gg, gu, gd)
    got_core = {}
    zorder = (4, 3, -3, 2, -2, 1, -1, 0)

    def grad_tiles(i):
        zz = rem(z + (8 + zorder[i]), 8)
        cols = pl.ds(mo(zz * 256, 256), 256)
        there = pl.ds(mo(zz * 256 + (1 - c) * 128, 128), 128)
        for w, rhs in ((0, feat), (1, feat), (2, cotf)):
            gbufs[w][:, cols] = (dot(lhs_t[w], rhs[:, cols]) * scale).astype(BF)
            got_core[w, i] = send(gbufs[w].at[:, there], coregot.at[w, i], core_dev)

    def mine_block(w, dz, part=None):
        zz = rem(z + (8 + dz), 8)
        cols = pl.ds(mo(zz * 256 + c * 128, 128), 128)
        rows = pl.ds(0, 512) if part is None else pl.ds(part * 256, 256)
        return gbufs[w].at[rows, cols]

    def core_sum(i):
        for w in range(3):
            got_core[w, i].wait_recv()
            add_into(mine_block(w, zorder[i]), coregot.at[w, i])

    def ring_grads():
        pend = {}
        for w in range(3):
            got_core[w, 0].wait_recv()
            add_into(mine_block(w, 4), coregot.at[w, 0])
            pend[w] = [
                send(mine_block(w, 4, k), zr.at[w, 0, k, pl.ds(0, 256)], z_dev(d))
                for k, d in ((0, 1), (1, -1))
            ]
        yield
        for n in (3, 2, 1):
            for w in range(3):
                new = []
                for k, d in ((0, 1), (1, -1)):
                    pend[w][k].wait_recv()
                    if n == 3:
                        add_into(mine_block(w, d * n, k), zr.at[w, 0, k, pl.ds(0, 256)])
                    else:
                        add_into(mine_block(w, d * n), zr.at[w, 3 - n, k])
                    new.append(send(mine_block(w, d * n), zr.at[w, 4 - n, k], z_dev(d)))
                pend[w] = new
                yield
        swaps = []
        for w in range(3):
            for copy in pend[w]:
                copy.wait_recv()
            add_into(mine_block(w, 0), zr.at[w, 3, 0], zr.at[w, 3, 1])
            swap = remote(mine_block(w, 0), swap_got.at[w], swap_dev)
            swaps.append(swap)

            @pl.when(jnp.logical_not(own_side))
            def _():
                swap.start()

            yield
        for w in range(3):
            swap = swaps[w]

            @pl.when(jnp.logical_not(own_side))
            def _():
                swap.wait()

            @pl.when(own_side)
            def _():
                swap_got[w] = mine_block(w, 0)[...]

            if w == 0:
                o_gate[...] = swap_got[w].T
            elif w == 1:
                o_up[...] = swap_got[w].T
            else:
                o_down[...] = swap_got[w]
            yield

    def run(flow, n=1):
        for _ in range(n):
            next(flow, None)

    def drain(flow):
        for _ in flow:
            pass

    scale = 1.0 / math.sqrt(8192.0)
    barrier = pltpu.get_barrier_semaphore()
    partners = [seq_dev(rem(s + d, 16)) for d in range(1, 16)]
    partners += [nb("y", 1), nb("y", -1), nb("x", 1), nb("x", -1), core_dev, swap_dev]
    for dev in partners:
        pl.semaphore_signal(barrier, inc=1, device_id=dev, device_id_type=MESH)
    inner[...] = dot(a1[...], x[...]).astype(BF)

    row = lax.broadcasted_iota(jnp.int32, (256, 512), 0)
    col = lax.broadcasted_iota(jnp.int32, (256, 512), 1)
    pick = (row == div(col, 32)).astype(F32).astype(BF)
    pick_t = (row == div(col, 32) * 16).astype(F32).astype(BF)
    diag = rem(lax.broadcasted_iota(jnp.int32, (512, 512), 0), 32) == rem(
        lax.broadcasted_iota(jnp.int32, (512, 512), 1), 32
    )

    def widen(cross, m, shift, picked):
        values = cross[...].astype(F32)
        for i in range(16):
            moved = values if i == 0 else pltpu.roll(values, 256 - i * shift, 1)
            turned[pl.ds(i * 32, 32), :] = moved.astype(BF)
        m[...] = jnp.where(diag, dot(turned[...], picked), 0.0).astype(BF)

    widen(c1, m1, 16, pick)
    pl.semaphore_wait(barrier, len(partners))

    got_inner = exchange(inner, spread)
    weights = ring_weights()
    run(weights)
    got_cot = share_core(cot, cotf)
    got_k = exchange(kk, kspread)
    widen(c2, m2, 16, pick)
    got_cot.wait_recv()
    cot_flow = gather_plane(cotf)
    run(cot_flow)
    run(weights)
    a1t[...] = a1[...].T
    got_inner()
    crossed[...] = dot(m1[...], spread[...]).astype(BF)
    got_k()
    scaled = (kspread[...].astype(F32) * crossed[...].astype(F32)).astype(BF)
    mixed[...] = dot(m2[...], scaled).astype(BF)
    got_mixed = exchange(mixed, mhome)
    run(cot_flow)
    run(weights, 3)
    a2t[...] = a2[...].T
    run(cot_flow)
    widen(c1, m1t, 1, pick_t)
    widen(c2, m2t, 1, pick_t)
    run(cot_flow)
    got_mixed()
    hid_in[...] = (x[...].astype(F32) + dot(a2[...], mhome[...])).astype(BF)
    got_feat = share_core(hid_in, feat)
    run(weights)
    got_feat.wait_recv()
    feat_flow = gather_plane(feat)
    run(feat_flow)
    run(cot_flow)
    run(weights, 2)
    run(feat_flow)
    run(cot_flow)
    run(weights, 1)
    run(feat_flow)
    drain(cot_flow)
    run(weights, 1)
    run(feat_flow)
    run(weights, 1)
    run(feat_flow)
    run(feat_flow)
    drain(weights)
    for j in range(2):
        cols = pl.ds(j * 256, 256)
        bh[:, cols] = dot_nt(cotf[...], wdf[cols, :])
    drain(feat_flow)

    for j in range(2):
        cols = pl.ds(j * 256, 256)
        gate = dot(feat[...], wgf[:, cols])
        up = dot(feat[...], wuf[:, cols])
        sig = 1.0 / (1.0 + jnp.exp(-gate))
        back = bh[:, cols]
        hid = (gate * sig * up).astype(BF)
        hidden[:, cols] = hid
        lhs_t[2, cols, :] = hid.T
        bg = (back * up * sig * (1.0 + gate * (1.0 - sig))).astype(BF)
        bgate[:, cols] = bg
        lhs_t[0, cols, :] = bg.T
        bu = (back * gate * sig).astype(BF)
        bup[:, cols] = bu
        lhs_t[1, cols, :] = bu.T
    grad_tiles(0)
    grad_tiles(1)
    grad_tiles(2)
    grads = ring_grads()
    run(grads)
    for j in range(8):
        rows = pl.ds(j * 256, 256)
        bt[:, rows] = (dot_nt(bgate[...], wgf[rows, :]) + dot_nt(bup[...], wuf[rows, :])).astype(BF)
    back_flow = scatter_plane(bt, 0)
    run(back_flow)
    core_sum(1)
    core_sum(2)
    for i in range(3, 8):
        grad_tiles(i)
    run(grads)
    run(back_flow)
    run(grads)
    run(back_flow)
    run(grads)
    run(back_flow, 2)
    for i in range(3, 8):
        core_sum(i)
    run(back_flow, 2)
    run(grads)
    run(back_flow, 2)
    run(grads)
    for j in range(8):
        cols = pl.ds(j * 256, 256)
        dt[:, cols] = dot(hidden[...], wdf[:, cols]).astype(BF)
    run(back_flow)
    run(grads)
    drain(back_flow)
    total[half_rows, :] = cot[half_rows, :].astype(F32) + bt[my_rows, my_cols].astype(F32)
    total[other_rows, :] = cot[other_rows, :].astype(F32) + rhome[0].astype(F32)
    bmix[...] = dot(a2t[...], total[...].astype(BF)).astype(BF)
    got_back = exchange(bmix, bspread)
    down_flow = scatter_plane(dt, 1)
    run(down_flow)
    run(grads)
    run(down_flow, 4)
    run(grads)
    got_back()
    bscaled = dot(m2t[...], bspread[...]).astype(BF).astype(F32)
    bcrossed = (bscaled * kspread[...].astype(F32)).astype(BF)
    binner[...] = dot(m1t[...], bcrossed).astype(BF)
    got_binner = exchange(binner, ihome)
    gks[...] = (bscaled * crossed[...].astype(F32)).astype(BF)
    got_gk = exchange(gks, gkhome)
    run(grads)
    run(down_flow, 5)
    run(grads)
    run(down_flow)
    got_binner()
    grad_in[...] = (total[...] + dot(a1t[...], ihome[...])).astype(BF)
    run(grads)
    got_gk()
    grad_k[...] = gkhome[...]
    drain(down_flow)
    out[half_rows, :] = (
        hid_in[half_rows, :].astype(F32) + dt[my_rows, my_cols].astype(F32)
    ).astype(BF)
    out[other_rows, :] = (hid_in[other_rows, :].astype(F32) + rhome[1].astype(F32)).astype(BF)
    drain(grads)
    for wait in sends:
        wait()
    assert count[0] <= N_SEM, count[0]


def hand_over(*refs):
    for i in range(6):
        refs[6 + i][...] = refs[i][...]


def per_device(*args):
    vm = pltpu.VMEM
    scratch = [
        vm((2048, 512), BF), vm((2048, 512), BF), vm((512, 2048), BF),
        vm((512, 2048), BF), vm((512, 2048), BF),
    ]
    scratch += [vm((512, 512), BF)] * 6
    scratch += [vm((512, 128), BF)] * 7
    scratch += [vm((512, 512), F32)] + [vm((512, 512), BF)] * 3
    scratch += [vm((512, 2048), BF)] * 2
    scratch += [vm((512, 2048), BF)] * 3
    scratch += [vm((3, 8, 512, 128), BF), vm((512, 256), BF), vm((3, 512, 512), BF)]
    scratch += [
        vm((3, 4, 2, 512, 128), BF), vm((3, 512, 128), BF),
        vm((2, 2, 4, 2, 64, 256), BF), vm((2, 2, 4, 2, 128, 256), BF),
        vm((2, 2, 2, 64, 256), BF), vm((2, 2, 2, 128, 256), BF),
        vm((2, 256, 128), BF), vm((512, 128), F32),
    ]
    scratch += [vm((512, 128), BF)] * 6
    scratch += [pltpu.SemaphoreType.DMA((N_SEM,)), pltpu.SemaphoreType.DMA((N_SEM,))]
    wide = jax.ShapeDtypeStruct((512, 128), BF)
    tall = jax.ShapeDtypeStruct((128, 512), BF)
    results = pl.pallas_call(
        layer_kernel,
        name="mixer_layer",
        out_shape=[wide, wide, wide, tall, tall, wide],
        in_specs=[pl.BlockSpec(memory_space=vm)] * 10,
        out_specs=[pl.BlockSpec(memory_space=vm)] * 6,
        scratch_shapes=scratch,
        compiler_params=pltpu.CompilerParams(
            collective_id=0, has_side_effects=True, vmem_limit_bytes=56 * MIB
        ),
    )(*args)
    return pl.pallas_call(
        hand_over,
        name="hand_over",
        out_shape=[wide, wide, wide, tall, tall, wide],
        in_specs=[pl.BlockSpec(memory_space=vm)] * 6,
        out_specs=[pl.BlockSpec(memory_space=vm)] * 6,
    )(*results)


def solution(mesh):
    return jax.shard_map(
        per_device,
        mesh=mesh,
        in_specs=(
            P("seq", "tp"),
            P("seq", "tp"),
            P("seq", None),
            P("seq", None),
            P("seq", None),
            P("seq", None),
            P("seq", "tp"),
            P("seq", "tp"),
            P("tp", "seq"),
            P("seq", "tp"),
        ),
        out_specs=(
            P("seq", "tp"),
            P("seq", "tp"),
            P("seq", "tp"),
            P("seq", "tp"),
            P("seq", "tp"),
            P("tp", "seq"),
        ),
        check_vma=False,
    )
```

```python
import math

import jax
import jax.numpy as jnp
from jax import lax
from jax.experimental import pallas as pl
from jax.experimental.pallas import tpu as pltpu
from jax.sharding import PartitionSpec as P

MESH = pl.DeviceIdType.MESH
BF = jnp.bfloat16
F32 = jnp.float32
MIB = 1 << 20
N_SEND = 10
N_RECV = 119


def dot(a, b):
    return jnp.dot(a, b, preferred_element_type=F32)


def dot_nt(a, b):
    return lax.dot_general(a, b, (((1,), (1,)), ((), ())), preferred_element_type=F32)


def rem(a, n):
    return lax.rem(a, jnp.int32(n))


def div(a, n):
    return lax.div(a, jnp.int32(n))


def mo(v, n):
    return pl.multiple_of(v, n)


def layer_kernel(
    x_in, k_in, a1_in, c1_in, c2_in, a2_in, wg, wu, wd, cot_in,
    out, grad_in, grad_k, o_gate, o_up, o_down,
    wgf, wuf, wdf, feat, cotf,
    m1, m1t, m2, m2t, a1t, a2t,
    inner, spread, kspread, crossed, mixed, mhome, hid_in,
    bh, hidden, bgate, bup, bt, dt,
    gg, gu, gd, coregot, turned, lhs_t,
    zr, swap_got, r1, r2, r3, r4, rhome, total,
    bmix, bspread, gks, binner, ihome, gkhome,
    x, kk, a1, c1, c2, a2, cot,
    ssem, rsem, lsem,
):
    s = lax.axis_index("seq")
    t = lax.axis_index("tp")
    z, h = div(s, 2), rem(s, 2)
    y, l, c = div(t, 4), rem(div(t, 2), 2), rem(t, 2)
    xx = h * 2 + l
    own_side = c == h

    def seq_dev(j):
        return {"seq": j, "tp": t}

    def z_dev(d):
        return {"seq": rem(z + (8 + d), 8) * 2 + h, "tp": t}

    def plane(yy, xp):
        return {"seq": z * 2 + div(xp, 2), "tp": yy * 4 + rem(xp, 2) * 2 + c}

    core_dev = {"seq": s, "tp": t + 1 - 2 * c}
    swap_dev = {"seq": z * 2 + 1 - h, "tp": t + 1 - 2 * c}

    def nb(axis, d):
        if axis == "y":
            return plane(rem(y + (4 + d), 4), xx)
        return plane(y, rem(xx + (4 + d), 4))

    recv_bytes, send_bytes, late = [], [], []

    def size(ref):
        return 2 * math.prod(ref.shape)

    def await_bytes(sem, n):
        view = wgf.at[pl.ds(0, n // 1024), :]
        pltpu.make_async_copy(view, view, sem).wait()

    def group():
        recv_bytes.append(0)
        return len(recv_bytes) - 1

    def wait(g):
        await_bytes(rsem.at[g], recv_bytes[g])

    def remote(src, dst, dev, g):
        if not send_bytes or send_bytes[-1] + size(src) > 2 * MIB:
            send_bytes.append(0)
        send_bytes[-1] += size(src)
        recv_bytes[g] += size(src)
        return pltpu.make_async_remote_copy(
            src, dst, ssem.at[len(send_bytes) - 1], rsem.at[g],
            device_id=dev, device_id_type=MESH,
        )

    def send(src, dst, dev, g):
        remote(src, dst, dev, g).start()

    def lone(src, dst, dev, k):
        return pltpu.make_async_remote_copy(
            src, dst, ssem.at[N_SEND + k], rsem.at[N_RECV + k],
            device_id=dev, device_id_type=MESH,
        )

    def exchange_order(i):
        k = div(i + 1, 2)
        return 8 + k * (2 * rem(i + 1, 2) - 1)

    n_exchange = [0]

    def exchange(src, dst):
        k = 8 + n_exchange[0]
        n_exchange[0] += 1

        def step(i, carry):
            j = rem(s + exchange_order(i), 16)
            pltpu.make_async_remote_copy(
                src.at[pl.ds(mo(j * 32, 32), 32)],
                dst.at[pl.ds(mo(s * 32, 32), 32)],
                ssem.at[N_SEND + k], rsem.at[N_RECV + k],
                device_id=seq_dev(j), device_id_type=MESH,
            ).start()
            return carry

        lax.fori_loop(0, 15, step, 0)
        mine = pl.ds(mo(s * 32, 32), 32)
        dst[mine, :] = src[mine, :]
        others = dst.at[pl.ds(0, 480), :]
        late.append(lambda: pltpu.make_async_copy(others, others, ssem.at[N_SEND + k]).wait())
        return lambda: pltpu.make_async_copy(others, others, rsem.at[N_RECV + k]).wait()

    def slot(ref, a, first, f, g, r0, nr):
        yy, xp = (f, g) if first == "y" else (g, f)
        rows = div(xp, 2) * 256 + (a * 128 + r0)
        cols = (yy * 2 + rem(xp, 2)) * 256
        return ref.at[pl.ds(mo(rows, 64), nr), pl.ds(mo(cols, 256), 256)]

    def axes_of(first):
        return (y, xx, "x") if first == "y" else (xx, y, "y")

    def gather_plane(buf):
        halves = ((0, "y"), (1, "x"))
        both = ((0, 1), (1, -1))
        st1, st2, fwd = {}, {}, {}

        def second(a, first, di):
            p1, p2, other = axes_of(first)
            f = rem(p1 + (4 + di), 4)
            piece = slot(buf, a, first, f, p2, 0, 128)
            st2[a, di] = group()
            for d in (1, -1):
                send(piece, piece, nb(other, d), st2[a, di])

        def second_forward(a, first, di):
            p1, p2, other = axes_of(first)
            f = rem(p1 + (4 + di), 4)
            wait(st2[a, di])
            st2[a, di] = group()
            for k, d in both:
                piece = slot(buf, a, first, f, rem(p2 + (4 - d), 4), k * 64, 64)
                send(piece, piece, nb(other, d), st2[a, di])

        for a, first in halves:
            p1, p2, _ = axes_of(first)
            piece = slot(buf, a, first, p1, p2, 0, 128)
            st1[a] = group()
            for d in (1, -1):
                send(piece, piece, nb(first, d), st1[a])
        for a, first in halves:
            second(a, first, 0)
        yield
        for a, first in halves:
            p1, p2, _ = axes_of(first)
            fwd[a] = group()
            wait(st1[a])
            for k, d in both:
                piece = slot(buf, a, first, rem(p1 + (4 - d), 4), p2, k * 64, 64)
                send(piece, piece, nb(first, d), fwd[a])
        for a, first in halves:
            second(a, first, -1)
            second(a, first, 1)
        yield
        for a, first in halves:
            second_forward(a, first, 0)
        yield
        for a, first in halves:
            wait(fwd[a])
            second(a, first, 2)
        yield
        for di in (-1, 1):
            for a, first in halves:
                second_forward(a, first, di)
        yield
        for a, first in halves:
            second_forward(a, first, 2)
        yield
        for di in (0, -1, 1, 2):
            for a, first in halves:
                wait(st2[a, di])

    def add_into(ref, *others):
        value = ref[...].astype(F32)
        for other in others:
            value = value + other[...].astype(F32)
        ref[...] = value.astype(BF)

    def scatter_plane(buf, w):
        halves = ((0, "x"), (1, "y"))
        both = ((0, 1), (1, -1))
        order = (2, 1, -1, 0)
        st1, st2, st3, st4 = {}, {}, {}, {}
        for gi, dg in enumerate(order):
            for a, first in halves:
                p1, p2, _ = axes_of(first)
                f, g = rem(p1 + 2, 4), rem(p2 + (4 + dg), 4)
                st1[a, gi] = group()
                for k, d in both:
                    piece = slot(buf, a, first, f, g, k * 64, 64)
                    send(piece, r1.at[w, a, gi, k], nb(first, d), st1[a, gi])
        yield
        for gi, dg in enumerate(order):
            for a, first in halves:
                p1, p2, _ = axes_of(first)
                g = rem(p2 + (4 + dg), 4)
                st2[a, gi] = group()
                wait(st1[a, gi])
                for k, d in both:
                    f = rem(p1 + (4 + d), 4)
                    add_into(slot(buf, a, first, f, g, k * 64, 64), r1.at[w, a, gi, k])
                    piece = slot(buf, a, first, f, g, 0, 128)
                    send(piece, r2.at[w, a, gi, k], nb(first, d), st2[a, gi])
            yield
        for gi, dg in enumerate(order):
            for a, first in halves:
                p1, p2, other = axes_of(first)
                g = rem(p2 + (4 + dg), 4)
                wait(st2[a, gi])
                add_into(
                    slot(buf, a, first, p1, g, 0, 128), r2.at[w, a, gi, 0], r2.at[w, a, gi, 1]
                )
                if dg == 2:
                    st3[a] = group()
                    for k, d in both:
                        piece = slot(buf, a, first, p1, g, k * 64, 64)
                        send(piece, r3.at[w, a, k], nb(other, d), st3[a])
            yield
        for a, first in halves:
            p1, p2, other = axes_of(first)
            st4[a] = group()
            wait(st3[a])
            for k, d in both:
                g = rem(p2 + (4 + d), 4)
                add_into(slot(buf, a, first, p1, g, k * 64, 64), r3.at[w, a, k])
                send(slot(buf, a, first, p1, g, 0, 128), r4.at[w, a, k], nb(other, d), st4[a])
        yield
        for a, first in halves:
            p1, p2, other = axes_of(first)
            wait(st4[a])
            add_into(slot(buf, a, first, p1, p2, 0, 128), r4.at[w, a, 0], r4.at[w, a, 1])
        rows = pl.ds(mo(h * 256, 256), 256)
        cols = pl.ds(mo((y * 2 + l) * 256 + (1 - c) * 128, 128), 128)
        back = group()
        send(buf.at[rows, cols], rhome.at[w], core_dev, back)
        yield
        wait(back)

    half_rows = pl.ds(mo(c * 256, 256), 256)
    other_rows = pl.ds(mo((1 - c) * 256, 256), 256)
    my_rows = pl.ds(mo(h * 256, 256), 256)
    my_cols = pl.ds(mo((y * 2 + l) * 256 + c * 128, 128), 128)

    def share_core(src, buf):
        g = group()
        send(src.at[other_rows], buf.at[my_rows, my_cols], core_dev, g)
        buf[my_rows, my_cols] = src[half_rows, :]
        return g

    def wslice(w, j, part=None):
        ref = (wdf, wgf, wuf)[w]
        if w == 0:
            rows = pl.ds(0, 512) if part is None else pl.ds(part * 256, 256)
            return ref.at[rows, pl.ds(mo(j * 128, 128), 128)]
        if part is None:
            return ref.at[pl.ds(mo(j * 128, 128), 128), :]
        return ref.at[pl.ds(mo(j * 128 + part * 64, 64), 64), :]

    wsrc = (wd, wg, wu)
    def ring_weights():
        swaps = [lone(wsrc[w], wslice(w, s), swap_dev, w) for w in range(3)]
        own = [pltpu.make_async_copy(wsrc[w], wslice(w, s), lsem.at[7 + w]) for w in range(3)]
        cores = [group() for w in range(3)]
        pend = [group() for w in range(3)]
        first = []
        for w in range(3):
            piece = wslice(w, z * 2 + c)
            first.append([remote(piece, piece, z_dev(d), pend[w]) for d in (1, -1)])
            first[w].append(remote(piece, piece, core_dev, cores[w]))

        @pl.when(jnp.logical_not(own_side))
        def _():
            for copy in swaps:
                copy.start()

        @pl.when(own_side)
        def _():
            for copy in own:
                copy.start()
            for w in range(3):
                own[w].wait()
                for copy in first[w]:
                    copy.start()

        def wait_swaps():
            @pl.when(jnp.logical_not(own_side))
            def _():
                for copy in swaps:
                    copy.wait_send()

        late.append(wait_swaps)
        yield

        def to_core(w, dz):
            piece = wslice(w, rem(z + (8 + dz), 8) * 2 + c)
            send(piece, piece, core_dev, cores[w])

        @pl.when(jnp.logical_not(own_side))
        def _():
            for w in range(3):
                swaps[w].wait_recv()
                for copy in first[w]:
                    copy.start()

        yield
        for k in (1, 2, 3):
            for w in range(3):
                wait(pend[w])
                pend[w] = group()
                for d in (1, -1):
                    part = None if k < 3 else (0 if d == 1 else 1)
                    piece = wslice(w, rem(z + (8 - d * k), 8) * 2 + c, part)
                    send(piece, piece, z_dev(d), pend[w])
                for d in (1, -1):
                    to_core(w, -d * k)
                yield
        for w in range(3):
            wait(pend[w])
            to_core(w, 4)
        yield
        for w in range(3):
            wait(cores[w])

    gbufs = (gg, gu, gd)
    got_core = {}
    zorder = (4, 3, -3, 2, -2, 1, -1, 0)

    def grad_tiles(i):
        zz = rem(z + (8 + zorder[i]), 8)
        cols = pl.ds(mo(zz * 256, 256), 256)
        there = pl.ds(mo(zz * 256 + (1 - c) * 128, 128), 128)
        got_core[i] = group()
        for w, rhs in ((0, feat), (1, feat), (2, cotf)):
            gbufs[w][:, cols] = (dot(lhs_t[w], rhs[:, cols]) * scale).astype(BF)
            send(gbufs[w].at[:, there], coregot.at[w, i], core_dev, got_core[i])

    def mine_block(w, dz, part=None):
        zz = rem(z + (8 + dz), 8)
        cols = pl.ds(mo(zz * 256 + c * 128, 128), 128)
        rows = pl.ds(0, 512) if part is None else pl.ds(part * 256, 256)
        return gbufs[w].at[rows, cols]

    def core_sum(i):
        wait(got_core[i])
        for w in range(3):
            add_into(mine_block(w, zorder[i]), coregot.at[w, i])

    def ring_grads():
        pend = {}
        wait(got_core[0])
        for w in range(3):
            add_into(mine_block(w, 4), coregot.at[w, 0])
            pend[w] = group()
            for k, d in ((0, 1), (1, -1)):
                send(mine_block(w, 4, k), zr.at[w, 0, k, pl.ds(0, 256)], z_dev(d), pend[w])
        yield
        for n in (3, 2, 1):
            for w in range(3):
                wait(pend[w])
                pend[w] = group()
                for k, d in ((0, 1), (1, -1)):
                    if n == 3:
                        add_into(mine_block(w, d * n, k), zr.at[w, 0, k, pl.ds(0, 256)])
                    else:
                        add_into(mine_block(w, d * n), zr.at[w, 3 - n, k])
                    send(mine_block(w, d * n), zr.at[w, 4 - n, k], z_dev(d), pend[w])
                yield
        swaps = [lone(mine_block(w, 0), swap_got.at[w], swap_dev, 3 + w) for w in range(3)]
        for w in range(3):
            wait(pend[w])
            add_into(mine_block(w, 0), zr.at[w, 3, 0], zr.at[w, 3, 1])

            @pl.when(jnp.logical_not(own_side))
            def _():
                swaps[w].start()

            yield
        for w in range(3):
            @pl.when(jnp.logical_not(own_side))
            def _():
                swaps[w].wait()

            @pl.when(own_side)
            def _():
                swap_got[w] = mine_block(w, 0)[...]

            if w == 0:
                o_gate[...] = swap_got[w].T
            elif w == 1:
                o_up[...] = swap_got[w].T
            else:
                o_down[...] = swap_got[w]
            yield

    def run(flow, n=1):
        for _ in range(n):
            next(flow, None)

    def drain(flow):
        for _ in flow:
            pass

    scale = 1.0 / math.sqrt(8192.0)
    fetch = [
        pltpu.make_async_copy(src, dst, lsem.at[i])
        for i, (src, dst) in enumerate(
            (
                (x_in, x), (a1_in, a1), (c1_in, c1), (cot_in, cot), (k_in, kk),
                (c2_in, c2), (a2_in, a2),
            )
        )
    ]
    for copy in fetch:
        copy.start()
    barrier = pltpu.get_barrier_semaphore()
    partners = [seq_dev(rem(s + d, 16)) for d in range(1, 16)]
    partners += [nb("y", 1), nb("y", -1), nb("x", 1), nb("x", -1), core_dev, swap_dev]
    for dev in partners:
        pl.semaphore_signal(barrier, inc=1, device_id=dev, device_id_type=MESH)
    fetch[0].wait()
    fetch[1].wait()
    inner[...] = dot(a1[...], x[...]).astype(BF)

    row = lax.broadcasted_iota(jnp.int32, (256, 512), 0)
    col = lax.broadcasted_iota(jnp.int32, (256, 512), 1)
    pick = (row == div(col, 32)).astype(F32).astype(BF)
    pick_t = (row == div(col, 32) * 16).astype(F32).astype(BF)
    diag = rem(lax.broadcasted_iota(jnp.int32, (512, 512), 0), 32) == rem(
        lax.broadcasted_iota(jnp.int32, (512, 512), 1), 32
    )

    def widen(cross, m, shift, picked):
        values = cross[...].astype(F32)
        for i in range(16):
            moved = values if i == 0 else pltpu.roll(values, 256 - i * shift, 1)
            turned[pl.ds(i * 32, 32), :] = moved.astype(BF)
        m[...] = jnp.where(diag, dot(turned[...], picked), 0.0).astype(BF)

    fetch[2].wait()
    widen(c1, m1, 16, pick)
    for copy in fetch[3:]:
        copy.wait()
    pl.semaphore_wait(barrier, len(partners))

    got_inner = exchange(inner, spread)
    weights = ring_weights()
    run(weights)
    got_cot = share_core(cot, cotf)
    got_k = exchange(kk, kspread)
    widen(c2, m2, 16, pick)
    wait(got_cot)
    cot_flow = gather_plane(cotf)
    run(cot_flow)
    run(weights)
    a1t[...] = a1[...].T
    got_inner()
    crossed[...] = dot(m1[...], spread[...]).astype(BF)
    got_k()
    scaled = (kspread[...].astype(F32) * crossed[...].astype(F32)).astype(BF)
    mixed[...] = dot(m2[...], scaled).astype(BF)
    got_mixed = exchange(mixed, mhome)
    run(cot_flow)
    run(weights, 3)
    a2t[...] = a2[...].T
    run(cot_flow)
    widen(c1, m1t, 1, pick_t)
    widen(c2, m2t, 1, pick_t)
    run(cot_flow)
    got_mixed()
    hid_in[...] = (x[...].astype(F32) + dot(a2[...], mhome[...])).astype(BF)
    got_feat = share_core(hid_in, feat)
    run(weights)
    wait(got_feat)
    feat_flow = gather_plane(feat)
    run(feat_flow)
    run(cot_flow)
    run(weights, 2)
    run(feat_flow)
    run(cot_flow)
    run(weights, 1)
    run(feat_flow)
    drain(cot_flow)
    run(weights, 1)
    run(feat_flow)
    run(weights, 1)
    run(feat_flow)
    run(feat_flow)
    drain(weights)
    for j in range(2):
        cols = pl.ds(j * 256, 256)
        bh[:, cols] = dot_nt(cotf[...], wdf[cols, :])
    drain(feat_flow)

    for j in range(2):
        cols = pl.ds(j * 256, 256)
        gate = dot(feat[...], wgf[:, cols])
        up = dot(feat[...], wuf[:, cols])
        sig = 1.0 / (1.0 + jnp.exp(-gate))
        back = bh[:, cols]
        hid = (gate * sig * up).astype(BF)
        hidden[:, cols] = hid
        lhs_t[2, cols, :] = hid.T
        bg = (back * up * sig * (1.0 + gate * (1.0 - sig))).astype(BF)
        bgate[:, cols] = bg
        lhs_t[0, cols, :] = bg.T
        bu = (back * gate * sig).astype(BF)
        bup[:, cols] = bu
        lhs_t[1, cols, :] = bu.T
    grad_tiles(0)
    grad_tiles(1)
    grad_tiles(2)
    grads = ring_grads()
    run(grads)
    for j in range(8):
        rows = pl.ds(j * 256, 256)
        bt[:, rows] = (dot_nt(bgate[...], wgf[rows, :]) + dot_nt(bup[...], wuf[rows, :])).astype(BF)
    back_flow = scatter_plane(bt, 0)
    run(back_flow)
    core_sum(1)
    core_sum(2)
    for i in range(3, 8):
        grad_tiles(i)
    run(grads)
    run(back_flow)
    run(grads)
    run(back_flow)
    run(grads)
    run(back_flow, 2)
    for i in range(3, 8):
        core_sum(i)
    run(back_flow, 2)
    run(grads)
    run(back_flow, 2)
    run(grads)
    for j in range(8):
        cols = pl.ds(j * 256, 256)
        dt[:, cols] = dot(hidden[...], wdf[:, cols]).astype(BF)
    run(back_flow)
    run(grads)
    drain(back_flow)
    total[half_rows, :] = cot[half_rows, :].astype(F32) + bt[my_rows, my_cols].astype(F32)
    total[other_rows, :] = cot[other_rows, :].astype(F32) + rhome[0].astype(F32)
    bmix[...] = dot(a2t[...], total[...].astype(BF)).astype(BF)
    got_back = exchange(bmix, bspread)
    down_flow = scatter_plane(dt, 1)
    run(down_flow)
    run(grads)
    run(down_flow, 4)
    run(grads)
    got_back()
    bscaled = dot(m2t[...], bspread[...]).astype(BF).astype(F32)
    bcrossed = (bscaled * kspread[...].astype(F32)).astype(BF)
    binner[...] = dot(m1t[...], bcrossed).astype(BF)
    got_binner = exchange(binner, ihome)
    gks[...] = (bscaled * crossed[...].astype(F32)).astype(BF)
    got_gk = exchange(gks, gkhome)
    run(grads)
    run(down_flow, 5)
    run(grads)
    run(down_flow)
    got_binner()
    grad_in[...] = (total[...] + dot(a1t[...], ihome[...])).astype(BF)
    run(grads)
    got_gk()
    grad_k[...] = gkhome[...]
    drain(down_flow)
    out[half_rows, :] = (
        hid_in[half_rows, :].astype(F32) + dt[my_rows, my_cols].astype(F32)
    ).astype(BF)
    out[other_rows, :] = (hid_in[other_rows, :].astype(F32) + rhome[1].astype(F32)).astype(BF)
    drain(grads)
    for finish in late:
        finish()
    for i, n in enumerate(send_bytes):
        await_bytes(ssem.at[i], n)
    assert len(send_bytes) == N_SEND, len(send_bytes)
    assert len(recv_bytes) == N_RECV, len(recv_bytes)


def hand_over(*refs):
    for i in range(6):
        refs[6 + i][...] = refs[i][...]


def per_device(*args):
    vm = pltpu.VMEM
    scratch = [
        vm((2048, 512), BF), vm((2048, 512), BF), vm((512, 2048), BF),
        vm((512, 2048), BF), vm((512, 2048), BF),
    ]
    scratch += [vm((512, 512), BF)] * 6
    scratch += [vm((512, 128), BF)] * 7
    scratch += [vm((512, 512), F32)] + [vm((512, 512), BF)] * 3
    scratch += [vm((512, 2048), BF)] * 2
    scratch += [vm((512, 2048), BF)] * 3
    scratch += [vm((3, 8, 512, 128), BF), vm((512, 256), BF), vm((3, 512, 512), BF)]
    scratch += [
        vm((3, 4, 2, 512, 128), BF), vm((3, 512, 128), BF),
        vm((2, 2, 4, 2, 64, 256), BF), vm((2, 2, 4, 2, 128, 256), BF),
        vm((2, 2, 2, 64, 256), BF), vm((2, 2, 2, 128, 256), BF),
        vm((2, 256, 128), BF), vm((512, 128), F32),
    ]
    scratch += [vm((512, 128), BF)] * 6
    scratch += [
        vm((512, 128), BF), vm((512, 128), BF), vm((512, 512), BF), vm((32, 256), BF),
        vm((32, 256), BF), vm((512, 512), BF), vm((512, 128), BF),
    ]
    scratch += [
        pltpu.SemaphoreType.DMA((N_SEND + 14,)), pltpu.SemaphoreType.DMA((N_RECV + 14,)),
        pltpu.SemaphoreType.DMA((10,)),
    ]
    wide = jax.ShapeDtypeStruct((512, 128), BF)
    tall = jax.ShapeDtypeStruct((128, 512), BF)
    results = pl.pallas_call(
        layer_kernel,
        name="mixer_layer",
        out_shape=[wide, wide, wide, tall, tall, wide],
        in_specs=[pl.BlockSpec(memory_space=pl.ANY)] * 10,
        out_specs=[pl.BlockSpec(memory_space=vm)] * 6,
        scratch_shapes=scratch,
        compiler_params=pltpu.CompilerParams(
            collective_id=0, has_side_effects=True, vmem_limit_bytes=56 * MIB
        ),
    )(*args)
    return pl.pallas_call(
        hand_over,
        name="hand_over",
        out_shape=[wide, wide, wide, tall, tall, wide],
        in_specs=[pl.BlockSpec(memory_space=vm)] * 6,
        out_specs=[pl.BlockSpec(memory_space=vm)] * 6,
    )(*results)


def solution(mesh):
    return jax.shard_map(
        per_device,
        mesh=mesh,
        in_specs=(
            P("seq", "tp"),
            P("seq", "tp"),
            P("seq", None),
            P("seq", None),
            P("seq", None),
            P("seq", None),
            P("seq", "tp"),
            P("seq", "tp"),
            P("tp", "seq"),
            P("seq", "tp"),
        ),
        out_specs=(
            P("seq", "tp"),
            P("seq", "tp"),
            P("seq", "tp"),
            P("seq", "tp"),
            P("seq", "tp"),
            P("tp", "seq"),
        ),
        check_vma=False,
    )
```

```python
import math

import jax
import jax.numpy as jnp
from jax import lax
from jax.experimental import pallas as pl
from jax.experimental.pallas import tpu as pltpu
from jax.sharding import PartitionSpec as P

MESH = pl.DeviceIdType.MESH
BF = jnp.bfloat16
F32 = jnp.float32
MIB = 1 << 20
FIRST = ("x1 w0 sc xk", "m2 c0 W t1", "cb C W W", "W t2 C mt", "C hm W f0", "C W W F", "C W F -C", "W F W F", "F W W bh", "W -F W gt", "W")
SECOND = ("ga g1 G bp", "B s1 g2 G", "B G B G", "B B s2 B", "B G B B", "G dp B G", "x3 D G D", "D D D G", "cx G D D", "D D D G", "D fi G fk", "fo -G")
N_SEND = 9
N_RECV = 119


def dot(a, b):
    return jnp.dot(a, b, preferred_element_type=F32)


def dot_nt(a, b):
    return lax.dot_general(a, b, (((1,), (1,)), ((), ())), preferred_element_type=F32)


def rem(a, n):
    return lax.rem(a, jnp.int32(n))


def div(a, n):
    return lax.div(a, jnp.int32(n))


def mo(v, n):
    return pl.multiple_of(v, n)


def layer_kernel(
    x_in, k_in, a1_in, c1_in, c2_in, a2_in, wg, wu, wd, cot_in,
    out, grad_in, grad_k, o_gate, o_up, o_down,
    wgf, wuf, wdf, acts,
    m1, m1t, m2, m2t, a1t, a2t,
    inner, spread, kspread, crossed, mixed, mhome, hid_in,
    bh, gates, hidden, bgate, bup, bt, dt,
    gall, coregot, turned, lhs_t,
    zr, swap_got, r1, r2, r3, r4, rhome, total,
    bmix, bspread, gks, binner, ihome, gkhome,
    x, kk, a1, c1, c2, a2, cot,
    ssem, rsem, lsem,
):
    feat, cotf = acts.at[0], acts.at[1]
    s = lax.axis_index("seq")
    t = lax.axis_index("tp")
    z, h = div(s, 2), rem(s, 2)
    y, l, c = div(t, 4), rem(div(t, 2), 2), rem(t, 2)
    xx = h * 2 + l
    own_side = c == h

    def seq_dev(j):
        return {"seq": j, "tp": t}

    def z_dev(d):
        return {"seq": rem(z + (8 + d), 8) * 2 + h, "tp": t}

    def plane(yy, xp):
        return {"seq": z * 2 + div(xp, 2), "tp": yy * 4 + rem(xp, 2) * 2 + c}

    core_dev = {"seq": s, "tp": t + 1 - 2 * c}
    swap_dev = {"seq": z * 2 + 1 - h, "tp": t + 1 - 2 * c}

    def nb(axis, d):
        if axis == "y":
            return plane(rem(y + (4 + d), 4), xx)
        return plane(y, rem(xx + (4 + d), 4))

    recv_bytes, send_bytes, late = [], [], []

    def size(ref):
        return 2 * math.prod(ref.shape)

    def await_bytes(sem, n):
        view = wgf.at[pl.ds(0, n // 1024), :]
        pltpu.make_async_copy(view, view, sem).wait()

    def group():
        recv_bytes.append(0)
        return len(recv_bytes) - 1

    def wait(g):
        await_bytes(rsem.at[g], recv_bytes[g])

    def remote(src, dst, dev, g):
        if not send_bytes or send_bytes[-1] + size(src) > 2 * MIB:
            send_bytes.append(0)
        send_bytes[-1] += size(src)
        recv_bytes[g] += size(src)
        return pltpu.make_async_remote_copy(
            src, dst, ssem.at[len(send_bytes) - 1], rsem.at[g],
            device_id=dev, device_id_type=MESH,
        )

    def send(src, dst, dev, g):
        remote(src, dst, dev, g).start()

    def lone(src, dst, dev, k):
        return pltpu.make_async_remote_copy(
            src, dst, ssem.at[N_SEND + k], rsem.at[N_RECV + k],
            device_id=dev, device_id_type=MESH,
        )

    n_exchange = [0]

    def exchange(src, dst):
        k = 8 + n_exchange[0]
        n_exchange[0] += 1

        for d in (8, 7, 9, 6, 10, 5, 11, 4, 12, 3, 13, 2, 14, 1, 15):
            j = rem(s + d, 16)
            pltpu.make_async_remote_copy(
                src.at[pl.ds(mo(j * 32, 32), 32)],
                dst.at[pl.ds(mo(s * 32, 32), 32)],
                ssem.at[N_SEND + k], rsem.at[N_RECV + k],
                device_id=seq_dev(j), device_id_type=MESH,
            ).start()
        mine = pl.ds(mo(s * 32, 32), 32)
        dst[mine, :] = src[mine, :]
        others = dst.at[pl.ds(0, 480), :]
        late.append(lambda: pltpu.make_async_copy(others, others, ssem.at[N_SEND + k]).wait())
        return lambda: pltpu.make_async_copy(others, others, rsem.at[N_RECV + k]).wait()

    def slot(ref, a, first, f, g, r0, nr):
        yy, xp = (f, g) if first == "y" else (g, f)
        rows = div(xp, 2) * 256 + (a * 128 + r0)
        cols = (yy * 2 + rem(xp, 2)) * 256
        return ref.at[pl.ds(mo(rows, 64), nr), pl.ds(mo(cols, 256), 256)]

    def axes_of(first):
        return (y, xx, "x") if first == "y" else (xx, y, "y")

    def gather_plane(buf):
        halves = ((0, "y"), (1, "x"))
        both = ((0, 1), (1, -1))
        st1, st2, fwd = {}, {}, {}

        def second(a, first, di):
            p1, p2, other = axes_of(first)
            f = rem(p1 + (4 + di), 4)
            piece = slot(buf, a, first, f, p2, 0, 128)
            st2[a, di] = group()
            for d in (1, -1):
                send(piece, piece, nb(other, d), st2[a, di])

        def second_forward(a, first, di):
            p1, p2, other = axes_of(first)
            f = rem(p1 + (4 + di), 4)
            wait(st2[a, di])
            st2[a, di] = group()
            for k, d in both:
                piece = slot(buf, a, first, f, rem(p2 + (4 - d), 4), k * 64, 64)
                send(piece, piece, nb(other, d), st2[a, di])

        for a, first in halves:
            p1, p2, _ = axes_of(first)
            piece = slot(buf, a, first, p1, p2, 0, 128)
            st1[a] = group()
            for d in (1, -1):
                send(piece, piece, nb(first, d), st1[a])
        for a, first in halves:
            second(a, first, 0)
        yield
        for a, first in halves:
            p1, p2, _ = axes_of(first)
            fwd[a] = group()
            wait(st1[a])
            for k, d in both:
                piece = slot(buf, a, first, rem(p1 + (4 - d), 4), p2, k * 64, 64)
                send(piece, piece, nb(first, d), fwd[a])
        for a, first in halves:
            second(a, first, -1)
            second(a, first, 1)
        yield
        for a, first in halves:
            second_forward(a, first, 0)
        yield
        for a, first in halves:
            wait(fwd[a])
            second(a, first, 2)
        yield
        for di in (-1, 1):
            for a, first in halves:
                second_forward(a, first, di)
        yield
        for a, first in halves:
            second_forward(a, first, 2)
        yield
        for di in (0, -1, 1, 2):
            for a, first in halves:
                wait(st2[a, di])

    def add_into(ref, *others):
        value = ref[...].astype(F32)
        for other in others:
            value = value + other[...].astype(F32)
        ref[...] = value.astype(BF)

    def scatter_plane(buf, w):
        halves = ((0, "x"), (1, "y"))
        both = ((0, 1), (1, -1))
        order = (2, 1, -1, 0)
        st1, st2, st3, st4 = {}, {}, {}, {}
        for gi, dg in enumerate(order):
            for a, first in halves:
                p1, p2, _ = axes_of(first)
                f, g = rem(p1 + 2, 4), rem(p2 + (4 + dg), 4)
                st1[a, gi] = group()
                for k, d in both:
                    piece = slot(buf, a, first, f, g, k * 64, 64)
                    send(piece, r1.at[w, a, gi, k], nb(first, d), st1[a, gi])
        yield
        for gi, dg in enumerate(order):
            for a, first in halves:
                p1, p2, _ = axes_of(first)
                g = rem(p2 + (4 + dg), 4)
                st2[a, gi] = group()
                wait(st1[a, gi])
                for k, d in both:
                    f = rem(p1 + (4 + d), 4)
                    add_into(slot(buf, a, first, f, g, k * 64, 64), r1.at[w, a, gi, k])
                    piece = slot(buf, a, first, f, g, 0, 128)
                    send(piece, r2.at[w, a, gi, k], nb(first, d), st2[a, gi])
            yield
        for gi, dg in enumerate(order):
            for a, first in halves:
                p1, p2, other = axes_of(first)
                g = rem(p2 + (4 + dg), 4)
                wait(st2[a, gi])
                add_into(
                    slot(buf, a, first, p1, g, 0, 128), r2.at[w, a, gi, 0], r2.at[w, a, gi, 1]
                )
                if dg == 2:
                    st3[a] = group()
                    for k, d in both:
                        piece = slot(buf, a, first, p1, g, k * 64, 64)
                        send(piece, r3.at[w, a, k], nb(other, d), st3[a])
            yield
        for a, first in halves:
            p1, p2, other = axes_of(first)
            st4[a] = group()
            wait(st3[a])
            for k, d in both:
                g = rem(p2 + (4 + d), 4)
                add_into(slot(buf, a, first, p1, g, k * 64, 64), r3.at[w, a, k])
                send(slot(buf, a, first, p1, g, 0, 128), r4.at[w, a, k], nb(other, d), st4[a])
        yield
        for a, first in halves:
            p1, p2, other = axes_of(first)
            wait(st4[a])
            add_into(slot(buf, a, first, p1, p2, 0, 128), r4.at[w, a, 0], r4.at[w, a, 1])
        rows = pl.ds(mo(h * 256, 256), 256)
        cols = pl.ds(mo((y * 2 + l) * 256 + (1 - c) * 128, 128), 128)
        back = group()
        send(buf.at[rows, cols], rhome.at[w], core_dev, back)
        yield
        wait(back)

    half_rows = pl.ds(mo(c * 256, 256), 256)
    other_rows = pl.ds(mo((1 - c) * 256, 256), 256)
    my_rows = pl.ds(mo(h * 256, 256), 256)
    my_cols = pl.ds(mo((y * 2 + l) * 256 + c * 128, 128), 128)

    def share_core(src, buf):
        g = group()
        send(src.at[other_rows], buf.at[my_rows, my_cols], core_dev, g)
        buf[my_rows, my_cols] = src[half_rows, :]
        return g

    def wslice(w, j, part=None):
        ref = (wdf, wgf, wuf)[w]
        if w == 0:
            rows = pl.ds(0, 512) if part is None else pl.ds(part * 256, 256)
            return ref.at[rows, pl.ds(mo(j * 128, 128), 128)]
        if part is None:
            return ref.at[pl.ds(mo(j * 128, 128), 128), :]
        return ref.at[pl.ds(mo(j * 128 + part * 64, 64), 64), :]

    wsrc = (wd, wg, wu)
    def ring_weights():
        swaps = [lone(wsrc[w], wslice(w, s), swap_dev, w) for w in range(3)]
        own = [pltpu.make_async_copy(wsrc[w], wslice(w, s), lsem.at[7 + w]) for w in range(3)]
        cores = [group() for w in range(3)]
        pend = [group() for w in range(3)]
        first = []
        for w in range(3):
            piece = wslice(w, z * 2 + c)
            first.append([remote(piece, piece, z_dev(d), pend[w]) for d in (1, -1)])
            first[w].append(remote(piece, piece, core_dev, cores[w]))

        @pl.when(jnp.logical_not(own_side))
        def _():
            for copy in swaps:
                copy.start()

        @pl.when(own_side)
        def _():
            for copy in own:
                copy.start()
            for w in range(3):
                own[w].wait()
                for copy in first[w]:
                    copy.start()

        def wait_swaps():
            @pl.when(jnp.logical_not(own_side))
            def _():
                for copy in swaps:
                    copy.wait_send()

        late.append(wait_swaps)
        yield

        def to_core(w, dz):
            piece = wslice(w, rem(z + (8 + dz), 8) * 2 + c)
            send(piece, piece, core_dev, cores[w])

        @pl.when(jnp.logical_not(own_side))
        def _():
            for w in range(3):
                swaps[w].wait_recv()
                for copy in first[w]:
                    copy.start()

        yield
        for k in (1, 2, 3):
            for w in range(3):
                wait(pend[w])
                pend[w] = group()
                for d in (1, -1):
                    part = None if k < 3 else (0 if d == 1 else 1)
                    piece = wslice(w, rem(z + (8 - d * k), 8) * 2 + c, part)
                    send(piece, piece, z_dev(d), pend[w])
                for d in (1, -1):
                    to_core(w, -d * k)
                yield
        for w in (0, 1):
            wait(pend[w])
            to_core(w, 4)
        yield
        wait(cores[0])
        yield
        wait(pend[2])
        to_core(2, 4)
        yield
        wait(cores[1])
        yield
        wait(cores[2])
        yield

    tile_sem = []

    def ring_place(i):
        return rem(z + (8 + (4, 3, -3, 2, -2, 1, -1, 0)[i]), 8)

    def grad_tiles(lo, hi):
        if not tile_sem:
            tile_sem.append(len(recv_bytes))
            recv_bytes.extend([3 * 512 * 128 * 2] * 8)
            for i in range(8):
                late.append(lambda i=i: await_bytes(ssem.at[N_SEND + 14 + i], 3 * 512 * 128 * 2))

        for i in range(lo, hi):
            zz = ring_place(i)
            cols = pl.ds(mo(zz * 256, 256), 256)
            there = pl.ds(mo(zz * 256 + (1 - c) * 128, 128), 128)
            for w in range(3):
                gall[w, :, cols] = (dot(lhs_t[w], acts[w // 2, :, cols]) * scale).astype(BF)
                pltpu.make_async_remote_copy(
                    gall.at[w, :, there], coregot.at[w, i],
                    ssem.at[N_SEND + 14 + i], rsem.at[tile_sem[0] + i],
                    device_id=core_dev, device_id_type=MESH,
                ).start()

    def mine_block(w, dz, part=None):
        zz = rem(z + (8 + dz), 8)
        cols = pl.ds(mo(zz * 256 + c * 128, 128), 128)
        rows = pl.ds(0, 512) if part is None else pl.ds(part * 256, 256)
        return gall.at[w, rows, cols]

    def core_sum(lo, hi):
        for i in range(lo, hi):
            await_bytes(rsem.at[tile_sem[0] + i], 3 * 512 * 128 * 2)
            cols = pl.ds(mo(ring_place(i) * 256 + c * 128, 128), 128)
            for w in range(3):
                add_into(gall.at[w, :, cols], coregot.at[w, i])

    def ring_grads():
        pend = {}
        core_sum(0, 1)
        for w in range(3):
            pend[w] = group()
            for k, d in ((0, 1), (1, -1)):
                send(mine_block(w, 4, k), zr.at[w, 0, k, pl.ds(0, 256)], z_dev(d), pend[w])
        yield
        for n in (3, 2, 1):
            for w in range(3):
                wait(pend[w])
                pend[w] = group()
                for k, d in ((0, 1), (1, -1)):
                    if n == 3:
                        add_into(mine_block(w, d * n, k), zr.at[w, 0, k, pl.ds(0, 256)])
                    else:
                        add_into(mine_block(w, d * n), zr.at[w, 3 - n, k])
                    send(mine_block(w, d * n), zr.at[w, 4 - n, k], z_dev(d), pend[w])
                yield
        swaps = [lone(mine_block(w, 0), swap_got.at[w], swap_dev, 3 + w) for w in range(3)]
        for w in range(3):
            wait(pend[w])
            add_into(mine_block(w, 0), zr.at[w, 3, 0], zr.at[w, 3, 1])

            @pl.when(jnp.logical_not(own_side))
            def _():
                swaps[w].start()

            yield
        for w in range(3):
            @pl.when(jnp.logical_not(own_side))
            def _():
                swaps[w].wait()

            @pl.when(own_side)
            def _():
                swap_got[w] = mine_block(w, 0)[...]

            if w == 0:
                o_gate[...] = swap_got[w].T
            elif w == 1:
                o_up[...] = swap_got[w].T
            else:
                o_down[...] = swap_got[w]
            yield

    def run(flow, n=1):
        for _ in range(n):
            next(flow, None)

    def drain(flow):
        for _ in flow:
            pass

    scale = 1.0 / math.sqrt(8192.0)
    fetch = [
        pltpu.make_async_copy(src, dst, lsem.at[i])
        for i, (src, dst) in enumerate(
            (
                (x_in, x), (a1_in, a1), (c1_in, c1), (cot_in, cot), (k_in, kk),
                (c2_in, c2), (a2_in, a2),
            )
        )
    ]
    for copy in fetch:
        copy.start()
    barrier = pltpu.get_barrier_semaphore()
    partners = [seq_dev(rem(s + d, 16)) for d in range(1, 16)]
    partners += [nb("y", 1), nb("y", -1), nb("x", 1), nb("x", -1), core_dev, swap_dev]
    for dev in partners:
        pl.semaphore_signal(barrier, inc=1, device_id=dev, device_id_type=MESH)
    fetch[0].wait()
    fetch[1].wait()
    inner[...] = dot(a1[...], x[...]).astype(BF)

    row = lax.broadcasted_iota(jnp.int32, (256, 512), 0)
    col = lax.broadcasted_iota(jnp.int32, (256, 512), 1)
    pick = (row == div(col, 32)).astype(F32).astype(BF)
    pick_t = (row == div(col, 32) * 16).astype(F32).astype(BF)
    diag = rem(lax.broadcasted_iota(jnp.int32, (512, 512), 0), 32) == rem(
        lax.broadcasted_iota(jnp.int32, (512, 512), 1), 32
    )

    def widen(cross, m, shift, picked):
        values = cross[...].astype(F32)
        for i in range(16):
            moved = values if i == 0 else pltpu.roll(values, 256 - i * shift, 1)
            turned[pl.ds(i * 32, 32), :] = moved.astype(BF)
        m[...] = jnp.where(diag, dot(turned[...], picked), 0.0).astype(BF)

    fetch[2].wait()
    widen(c1, m1, 16, pick)
    for copy in fetch[3:]:
        copy.wait()
    pl.semaphore_wait(barrier, len(partners))

    flows = {}
    got = {}

    def start_mix():
        got["inner"] = exchange(inner, spread)

    def start_weights():
        flows["W"] = ring_weights()
        run(flows["W"])

    def share_cot():
        got["cot"] = share_core(cot, cotf)

    def start_k():
        got["k"] = exchange(kk, kspread)

    def widen_second():
        widen(c2, m2, 16, pick)

    def start_cot():
        wait(got["cot"])
        flows["C"] = gather_plane(cotf)
        run(flows["C"])

    def turn_first():
        a1t[...] = a1[...].T

    def turn_second():
        a2t[...] = a2[...].T

    def cross_blocks():
        got["inner"]()
        crossed[...] = dot(m1[...], spread[...]).astype(BF)
        got["k"]()
        scaled = (kspread[...].astype(F32) * crossed[...].astype(F32)).astype(BF)
        mixed[...] = dot(m2[...], scaled).astype(BF)
        got["mixed"] = exchange(mixed, mhome)

    def widen_turned():
        widen(c1, m1t, 1, pick_t)
        widen(c2, m2t, 1, pick_t)

    def home():
        got["mixed"]()
        hid_in[...] = (x[...].astype(F32) + dot(a2[...], mhome[...])).astype(BF)
        got["feat"] = share_core(hid_in, feat)

    def start_feat():
        wait(got["feat"])
        flows["F"] = gather_plane(feat)
        run(flows["F"])

    def back_hidden():
        for j in range(2):
            cols = pl.ds(mo(j * 256, 256), 256)
            bh[:, cols] = dot_nt(cotf[...], wdf[cols, :])

    def gate_product():
        for j in range(2):
            cols = pl.ds(mo(j * 256, 256), 256)
            gates[:, cols] = dot(feat[...], wgf[:, cols])

    def gated():
        for j in range(2):
            cols = pl.ds(mo(j * 256, 256), 256)
            gate = gates[:, cols]
            up = dot(feat[...], wuf[:, cols])
            sig = 1.0 / (1.0 + jnp.exp(-gate))
            back = bh[:, cols]
            hid = (gate * sig * up).astype(BF)
            hidden[:, cols] = hid
            lhs_t[2, cols, :] = hid.T
            bg = (back * up * sig * (1.0 + gate * (1.0 - sig))).astype(BF)
            bgate[:, cols] = bg
            lhs_t[0, cols, :] = bg.T
            bu = (back * gate * sig).astype(BF)
            bup[:, cols] = bu
            lhs_t[1, cols, :] = bu.T

        flows["G"] = ring_grads()

    def back_product():
        for j in range(8):
            rows = pl.ds(mo(j * 256, 256), 256)
            bt[:, rows] = (
                dot_nt(bgate[...], wgf[rows, :]) + dot_nt(bup[...], wuf[rows, :])
            ).astype(BF)

        flows["B"] = scatter_plane(bt, 0)

    def down_product():
        for j in range(8):
            cols = pl.ds(mo(j * 256, 256), 256)
            dt[:, cols] = dot(hidden[...], wdf[:, cols]).astype(BF)

        flows["D"] = scatter_plane(dt, 1)

    def back_home():
        drain(flows["B"])
        total[half_rows, :] = cot[half_rows, :].astype(F32) + bt[my_rows, my_cols].astype(F32)
        total[other_rows, :] = cot[other_rows, :].astype(F32) + rhome[0].astype(F32)
        bmix[...] = dot(a2t[...], total[...].astype(BF)).astype(BF)
        got["back"] = exchange(bmix, bspread)

    def cross_back():
        got["back"]()
        bscaled = dot(m2t[...], bspread[...]).astype(BF).astype(F32)
        bcrossed = (bscaled * kspread[...].astype(F32)).astype(BF)
        binner[...] = dot(m1t[...], bcrossed).astype(BF)
        got["binner"] = exchange(binner, ihome)
        gks[...] = (bscaled * crossed[...].astype(F32)).astype(BF)
        got["gk"] = exchange(gks, gkhome)

    def finish_inputs():
        got["binner"]()
        grad_in[...] = (total[...] + dot(a1t[...], ihome[...])).astype(BF)

    def finish_kernel():
        got["gk"]()
        grad_k[...] = gkhome[...]

    def finish_output():
        drain(flows["D"])
        out[half_rows, :] = (
            hid_in[half_rows, :].astype(F32) + dt[my_rows, my_cols].astype(F32)
        ).astype(BF)
        out[other_rows, :] = (
            hid_in[other_rows, :].astype(F32) + rhome[1].astype(F32)
        ).astype(BF)

    steps = {
        "x1": start_mix, "w0": start_weights, "sc": share_cot, "xk": start_k,
        "m2": widen_second, "c0": start_cot, "t1": turn_first, "t2": turn_second,
        "cb": cross_blocks, "mt": widen_turned, "hm": home, "f0": start_feat,
        "bh": back_hidden, "ga": gated, "gt": gate_product, "bp": back_product, "dp": down_product,
        "x3": back_home, "cx": cross_back, "fi": finish_inputs, "fk": finish_kernel,
        "fo": finish_output,
        "g1": lambda: grad_tiles(0, 3), "g2": lambda: grad_tiles(3, 8),
        "s1": lambda: core_sum(1, 3), "s2": lambda: core_sum(3, 8),
    }
    for line in FIRST + SECOND:
        for name in line.split():
            if name in steps:
                steps[name]()
            elif name[0] == "-":
                drain(flows[name[1]])
            else:
                run(flows[name])
    for finish in late:
        finish()
    for i, n in enumerate(send_bytes):
        await_bytes(ssem.at[i], n)
    assert len(send_bytes) == N_SEND, len(send_bytes)
    assert len(recv_bytes) == N_RECV, len(recv_bytes)


def hand_over(*refs):
    for i in range(6):
        refs[6 + i][...] = refs[i][...]


def per_device(*args):
    vm = pltpu.VMEM
    scratch = [
        vm((2048, 512), BF), vm((2048, 512), BF), vm((512, 2048), BF),
        vm((2, 512, 2048), BF),
    ]
    scratch += [vm((512, 512), BF)] * 6
    scratch += [vm((512, 128), BF)] * 7
    scratch += [vm((512, 512), F32)] * 2 + [vm((512, 512), BF)] * 3
    scratch += [vm((512, 2048), BF)] * 2
    scratch += [vm((3, 512, 2048), BF)]
    scratch += [vm((3, 8, 512, 128), BF), vm((512, 256), BF), vm((3, 512, 512), BF)]
    scratch += [
        vm((3, 4, 2, 512, 128), BF), vm((3, 512, 128), BF),
        vm((2, 2, 4, 2, 64, 256), BF), vm((2, 2, 4, 2, 128, 256), BF),
        vm((2, 2, 2, 64, 256), BF), vm((2, 2, 2, 128, 256), BF),
        vm((2, 256, 128), BF), vm((512, 128), F32),
    ]
    scratch += [vm((512, 128), BF)] * 6
    scratch += [
        vm((512, 128), BF), vm((512, 128), BF), vm((512, 512), BF), vm((32, 256), BF),
        vm((32, 256), BF), vm((512, 512), BF), vm((512, 128), BF),
    ]
    scratch += [
        pltpu.SemaphoreType.DMA((N_SEND + 22,)), pltpu.SemaphoreType.DMA((N_RECV + 14,)),
        pltpu.SemaphoreType.DMA((10,)),
    ]
    wide = jax.ShapeDtypeStruct((512, 128), BF)
    tall = jax.ShapeDtypeStruct((128, 512), BF)
    results = pl.pallas_call(
        layer_kernel,
        name="mixer_layer",
        out_shape=[wide, wide, wide, tall, tall, wide],
        in_specs=[pl.BlockSpec(memory_space=pl.ANY)] * 10,
        out_specs=[pl.BlockSpec(memory_space=vm)] * 6,
        scratch_shapes=scratch,
        compiler_params=pltpu.CompilerParams(
            collective_id=0, has_side_effects=True, vmem_limit_bytes=56 * MIB
        ),
    )(*args)
    return pl.pallas_call(
        hand_over,
        name="hand_over",
        out_shape=[wide, wide, wide, tall, tall, wide],
        in_specs=[pl.BlockSpec(memory_space=vm)] * 6,
        out_specs=[pl.BlockSpec(memory_space=vm)] * 6,
    )(*results)


def solution(mesh):
    return jax.shard_map(
        per_device,
        mesh=mesh,
        in_specs=(
            P("seq", "tp"),
            P("seq", "tp"),
            P("seq", None),
            P("seq", None),
            P("seq", None),
            P("seq", None),
            P("seq", "tp"),
            P("seq", "tp"),
            P("tp", "seq"),
            P("seq", "tp"),
        ),
        out_specs=(
            P("seq", "tp"),
            P("seq", "tp"),
            P("seq", "tp"),
            P("seq", "tp"),
            P("seq", "tp"),
            P("tp", "seq"),
        ),
        check_vma=False,
    )
```
